512 devices in a mesh: req: 32 (over z, core), head: 4 (over y), row: 4 (over x).
Axes of the slice: x: 4, y: 4, z: 16, core: 2. Of those that a mesh axis runs over, the one named last changes fastest.
Arguments:
- incoming_activations: bfloat16 [512, 4, 2048], P(('req', 'head'), None, 'row'), may hold values from -6 to 6
- genuine_symbol_number: int32 [512], replicated, may hold values from 1 to 4, as said below
- caller_sheet_slot: int32 [512], replicated, may hold values from 0 to 511, as said below
- memory_sheets: float32 [512, 32, 4096], P('req', 'head', 'row'), may hold values from -4 to 4
- prior_activation_sheets: float32 [512, 2048], P('req', 'row'), may hold values from -6 to 6
- blend_fractions: float32 [5, 2048], P(None, 'row'), may hold values from 0 to 1
- first_projectors: bfloat16 [3, 2048, 2048], P(None, 'row', 'head'), may hold values from -0.125 to 0.125
- fading_narrow_projector: bfloat16 [2048, 96], P('row'), may hold values from -0.125 to 0.125
- fading_widen_projector: bfloat16 [96, 2048], P(None, 'head'), may hold values from -0.625 to 0.625
- fading_offset: float32 [2048], P('head'), may hold values from -5 to 1
- context_step_narrowing: bfloat16 [2048, 96], P('row'), may hold values from -0.125 to 0.125
- context_step_widening: bfloat16 [96, 2048], P(None, 'head'), may hold values from -0.625 to 0.625
- context_step_offset: float32 [2048], P('head'), may hold values from -2 to 2
- erasure_address_gain: float32 [2048], P('head'), may hold values from 0.25 to 2
- address_correction: float32 [2048], P('head'), may hold values from 0 to 1.5
- reward_coefficients: float32 [32, 64], P('head'), may hold values from -0.6 to 0.6
- groupwise_gain: float32 [32, 64], P('head', 'row'), may hold values from 0.5 to 1.5
- final_projector: bfloat16 [32, 64, 2048], P('head', 'row'), may hold values from -0.125 to 0.125
Outputs:
- mixed: bfloat16 [512, 4, 2048], P(('req', 'head'), None, 'row')
- new_state: float32 [512, 32, 4096], P('req', 'head', 'row')
- new_shift: float32 [512, 2048], P('req', 'row')
The draws below stay inside these ranges and needn't reach their ends.
Inputs may be any that keep to these rules, and one draw needn't show every extreme that they name: `genuine_symbol_number`: every request has 1 or 4 valid tokens; the share with 4 differs between indices of req. `caller_sheet_slot`: a permutation; the pages of index i of req are i * 16 to (i + 1) * 16 - 1; for any two indices of req, between 0 and 1 of the first one's requests have their pages on the second.
All inputs are finite; a program needn't handle non-finite values.
Results may differ from the reference program's by a relative error of at most 0.02.
Values may be sent and summed in bfloat16 or wider, within the bound.
No kernel may reach another device: no remote copies, remote signals or barrier semaphores. Data moves between devices by JAX's collectives and lax.ppermute only.
A program may use at most 64 MiB of HBM per device.

```python
import jax
import jax.numpy as jnp
from jax import lax

D = 2048
GROUP_NUMBER = 32
CHANNEL_SPAN = 64
DL = 96
AL = 96
TS = 4
REQ_DEV = 16
REQ = 512


def draw_genuine_symbol_number(key, part):
    groups = REQ // REQ_DEV
    key_share, key_roll, key_fixed = jax.random.split(key, 3)
    long_share = jax.random.randint(key_share, (groups, 1), 0, 9)
    dice_roll = jax.random.randint(key_roll, (groups, REQ_DEV), 0, 8)
    counts = jnp.where(dice_roll < long_share, TS, 1).reshape(-1).astype(jnp.int32)
    chosen = jax.random.randint(key_fixed, (), 0, REQ)
    counts = counts.at[chosen].set(TS)
    counts = counts.at[(chosen + 1) % REQ].set(1)
    return counts


def shuffled(subkey):
    return jax.random.permutation(subkey, REQ_DEV)


def draw_caller_sheet_slot(key, part):
    groups = REQ // REQ_DEV
    key_owner, key_offset, key_rows, key_slots = jax.random.split(key, 4)
    owners = jax.random.permutation(key_owner, groups)
    offsets = jax.random.permutation(key_offset, groups)
    row_perm = jax.vmap(shuffled)(jax.random.split(key_rows, groups))
    slot_perm = jax.vmap(shuffled)(jax.random.split(key_slots, groups))
    device = jnp.arange(groups)[:, None]
    column = jnp.arange(REQ_DEV)[None, :]
    source = owners[(offsets[device] + column) % groups]
    slot_of = slot_perm[source, column]
    pages = (source * REQ_DEV + slot_of).astype(jnp.int32)
    request = device * REQ_DEV + row_perm
    return jnp.zeros((REQ,), jnp.int32).at[request.reshape(-1)].set(pages.reshape(-1))


def level_of(key, extent, pieces, smallest, largest):
    loudness, own = 1.0, jax.random.fold_in(key, 6)
    for axis_at, blocks in pieces:
        heights = jnp.exp(jax.random.uniform(jax.random.fold_in(own, axis_at), (blocks,), jnp.float32, smallest / len(pieces), largest / len(pieces)))
        loudness = loudness * jnp.repeat(heights, extent[axis_at] // blocks).reshape([-1 if axis == axis_at else 1 for axis in range(len(extent))])
    return loudness


def noise(key, shape, spread, bound, cuts=(), held_as=jnp.bfloat16):
    values = jax.random.normal(key, shape, jnp.float32) * spread
    if len(cuts) > 0:
        values = level_of(key, shape, cuts, -0.22, 0.18) * values
    return jnp.clip(values, min=-bound, max=bound).astype(held_as)


def setup_inputs(seed: int = 0) -> dict:
    key_list = jax.random.split(jax.random.key(seed), 19)
    return {
        "incoming_activations": noise(key_list[0], (REQ, TS, D), 1.0, 6.0, ((0, 128), (2, 4))),
        "genuine_symbol_number": draw_genuine_symbol_number(jax.random.fold_in(key_list[18], 71), 0),
        "caller_sheet_slot": draw_caller_sheet_slot(jax.random.fold_in(key_list[18], 71), 0),
        "memory_sheets": noise(key_list[3], (REQ, GROUP_NUMBER, CHANNEL_SPAN * CHANNEL_SPAN), 0.5, 4.0, ((0, 32), (1, 4), (2, 4)), jnp.float32),
        "prior_activation_sheets": noise(key_list[4], (REQ, D), 1.0, 6.0, ((0, 32), (1, 4)), jnp.float32),
        "blend_fractions": jnp.clip(1.0 * jax.random.uniform(key_list[5], (5, D), jnp.float32) ** level_of(key_list[5], (5, D), ((1, 4),), -0.2, 0.2), 0.0, 1.0),
        "first_projectors": noise(key_list[6], (3, D, D), D ** -0.5, 0.125, ((1, 4), (2, 4))),
        "fading_narrow_projector": noise(key_list[7], (D, DL), D ** -0.5, 0.125, ((0, 4),)),
        "fading_widen_projector": noise(key_list[8], (DL, D), DL ** -0.5, 0.625, ((1, 4),)),
        "fading_offset": jnp.clip(-5.0 + 6.0 * jax.random.uniform(key_list[9], (D,), jnp.float32) ** level_of(key_list[9], (D,), ((0, 4),), -0.2, 0.2), -5.0, 1.0),
        "context_step_narrowing": noise(key_list[10], (D, AL), D ** -0.5, 0.125, ((0, 4),)),
        "context_step_widening": noise(key_list[11], (AL, D), AL ** -0.5, 0.625, ((1, 4),)),
        "context_step_offset": jnp.clip(jax.random.uniform(key_list[12], (D,), jnp.float32, -2.0, 2.0) * level_of(key_list[12], (D,), ((0, 4),), -0.4, 0.0), -2.0, 2.0),
        "erasure_address_gain": jnp.clip(0.25 + 1.75 * jax.random.uniform(key_list[13], (D,), jnp.float32) ** level_of(key_list[13], (D,), ((0, 4),), -0.2, 0.2), 0.25, 2.0),
        "address_correction": jnp.clip(1.5 * jax.random.uniform(key_list[14], (D,), jnp.float32) ** level_of(key_list[14], (D,), ((0, 4),), -0.2, 0.2), 0.0, 1.5),
        "reward_coefficients": noise(key_list[15], (GROUP_NUMBER, CHANNEL_SPAN), 0.1, 0.6, ((0, 4),), jnp.float32),
        "groupwise_gain": jnp.clip(0.5 + 1.0 * jax.random.uniform(key_list[16], (GROUP_NUMBER, CHANNEL_SPAN), jnp.float32) ** level_of(key_list[16], (GROUP_NUMBER, CHANNEL_SPAN), ((0, 4), (1, 4)), -0.2, 0.2), 0.5, 1.5),
        "final_projector": noise(key_list[17], (GROUP_NUMBER, CHANNEL_SPAN, D), (GROUP_NUMBER * CHANNEL_SPAN) ** -0.5, 0.125, ((0, 4), (1, 4))),
    }


def project(rows, weight):
    flat = rows.reshape(-1, rows.shape[-1])
    result = jnp.dot(flat, weight, preferred_element_type=jnp.float32)
    return result.reshape(rows.shape[:-1] + (weight.shape[-1],))

def reference(incoming_activations, genuine_symbol_number, caller_sheet_slot, memory_sheets, prior_activation_sheets, blend_fractions, first_projectors, fading_narrow_projector, fading_widen_projector, fading_offset, context_step_narrowing, context_step_widening, context_step_offset, erasure_address_gain, address_correction, reward_coefficients, groupwise_gain, final_projector):
    state_now = memory_sheets[caller_sheet_slot].reshape(REQ, GROUP_NUMBER, CHANNEL_SPAN, CHANNEL_SPAN)
    shift_row = prior_activation_sheets[caller_sheet_slot]
    current = incoming_activations.astype(jnp.float32)
    before = jnp.concatenate([shift_row[:, None, :], current[:, :-1, :]], axis=1)
    towards = before - current
    mixed_in = [(current + towards * blend_fractions[branch]).astype(jnp.bfloat16) for branch in range(5)]
    acceptance_query = project(mixed_in[0], first_projectors[0])
    key_vec = project(mixed_in[2], first_projectors[1])
    payload_entries = project(mixed_in[3], first_projectors[2])
    decay_low = jnp.tanh(project(mixed_in[1], fading_narrow_projector)).astype(jnp.bfloat16)
    log_rate = -jax.nn.softplus(-(fading_offset + project(decay_low, fading_widen_projector))) - 0.5
    decay_rate = jnp.exp(-jnp.exp(log_rate))
    learn_low = project(mixed_in[4], context_step_narrowing).astype(jnp.bfloat16)
    learn_rate = jax.nn.sigmoid(context_step_offset + project(learn_low, context_step_widening))
    heads_shape = (REQ, TS, GROUP_NUMBER, CHANNEL_SPAN)
    scaled = (key_vec * erasure_address_gain).reshape(heads_shape)
    key_dir = scaled / jnp.sqrt(lax.optimization_barrier(jnp.sum(scaled * scaled, axis=-1, keepdims=True)) + 1e-06)
    address_corrected = (key_vec * (1.0 + (learn_rate - 1.0) * address_correction)).reshape(heads_shape)
    acceptance_query = acceptance_query.reshape(heads_shape)
    payload_entries = payload_entries.reshape(heads_shape)
    decay_rate = decay_rate.reshape(heads_shape)
    learn_rate = learn_rate.reshape(heads_shape)
    outputs = []
    for position in range(TS):
        live_now = (position < genuine_symbol_number)[:, None, None, None]
        removed = lax.optimization_barrier(jnp.sum(state_now * (-key_dir[:, position])[:, :, None, :], axis=-1))
        update = state_now * decay_rate[:, position][:, :, None, :]
        update = update + removed[..., None] * (key_dir[:, position] * learn_rate[:, position])[:, :, None, :]
        update = update + payload_entries[:, position][..., None] * address_corrected[:, position][:, :, None, :]
        state_now = jnp.where(live_now, update, state_now)
        reading = lax.optimization_barrier(jnp.sum(state_now * acceptance_query[:, position][:, :, None, :], axis=-1))
        outputs.append(jnp.where(live_now[..., 0], reading, jnp.zeros_like(reading)))
    groupwise_results = jnp.stack(outputs, axis=1)
    genuine_symbol_filter = (jnp.arange(TS)[None, :] < genuine_symbol_number[:, None])[:, :, None, None]
    reward_multiplier = lax.optimization_barrier(jnp.sum(acceptance_query * address_corrected * reward_coefficients, axis=-1, keepdims=True))
    reward_summand = jnp.where(genuine_symbol_filter, reward_multiplier * payload_entries, jnp.zeros_like(payload_entries))
    demeaned_entries = lax.optimization_barrier(jnp.mean(groupwise_results, axis=-1, keepdims=True))
    groupwise_spread = lax.optimization_barrier(jnp.mean((groupwise_results - demeaned_entries) * (groupwise_results - demeaned_entries), axis=-1, keepdims=True))
    standardised_groups = ((groupwise_results - demeaned_entries) / jnp.sqrt(groupwise_spread + 0.00064) * groupwise_gain + reward_summand).astype(jnp.bfloat16)
    mixed = project(standardised_groups.reshape(REQ, TS, GROUP_NUMBER * CHANNEL_SPAN), final_projector.reshape(GROUP_NUMBER * CHANNEL_SPAN, D)).astype(jnp.bfloat16)
    last_token = jnp.take_along_axis(current, (genuine_symbol_number - 1).astype(jnp.int32)[:, None, None], axis=1)[:, 0]
    new_state = jnp.zeros((REQ, GROUP_NUMBER, CHANNEL_SPAN * CHANNEL_SPAN), jnp.float32).at[caller_sheet_slot].set(state_now.reshape(REQ, GROUP_NUMBER, CHANNEL_SPAN * CHANNEL_SPAN))
    new_shift = jnp.zeros((REQ, D), jnp.float32).at[caller_sheet_slot].set(last_token)
    return (mixed, new_state, new_shift)
```

```python
import functools

import jax
import jax.numpy as jnp
import numpy as np
from jax import lax
from jax.experimental import pallas as pl
from jax.experimental.pallas import tpu as pltpu
from jax.sharding import PartitionSpec as P

CHANNEL_SPAN = 64
TS = 4
REQ_DEV = 16
HEADS = 8
ROWS = 16
FEATS = HEADS * CHANNEL_SPAN
VALS = HEADS * ROWS
TOK = REQ_DEV * TS
LANES = 128
DECAY_AT = 2 * FEATS + VALS
LEARN_AT = DECAY_AT + LANES
WIDTH = LEARN_AT + LANES
F32 = jnp.float32
BF16 = jnp.bfloat16
VMEM = pl.BlockSpec(memory_space=pltpu.VMEM)
SMEM = pl.BlockSpec(memory_space=pltpu.SMEM)


def value_lane(head, row):
    return (row % 2) * 64 + head * 8 + row // 2


def constant_matrices():
    lanes = np.arange(256)
    halves = (lanes[:, None] // 64 == lanes[None, :] // 64).astype(np.float32)
    c = np.arange(VALS)
    lane_head = (c % 64) // 8
    same_head = (lane_head[:, None] == lane_head[None, :]).astype(np.float32)
    head_to_lanes = (np.arange(FEATS)[:, None] // 64 == lane_head[None, :]).astype(np.float32)
    to_natural = np.zeros((VALS, VALS), np.float32)
    spread_values = np.zeros((FEATS, FEATS), np.float32)
    for head in range(HEADS):
        for row in range(ROWS):
            to_natural[value_lane(head, row), head * ROWS + row] = 1
            for part in range(4):
                spread_values[head * 64 + part * ROWS + row, part * VALS + value_lane(head, row)] = 1
    return halves, same_head, head_to_lanes, to_natural, spread_values


def dot(a, b):
    return jnp.dot(a, b, preferred_element_type=F32)


def dot_split(a, b):
    high = a.astype(BF16)
    low = (a - high.astype(F32)).astype(BF16)
    return dot(high, b) + dot(low, b)


def call(kernel, outs, in_specs, args, scratch=(), flops=0, name=None):
    size = sum(int(np.prod(a.shape)) * a.dtype.itemsize for a in args)
    size += sum(int(np.prod(o.shape)) * o.dtype.itemsize for o in outs)
    single = len(outs) == 1
    return pl.pallas_call(
        kernel,
        out_shape=outs[0] if single else outs,
        in_specs=in_specs,
        out_specs=VMEM if single else [VMEM] * len(outs),
        scratch_shapes=list(scratch),
        cost_estimate=pl.CostEstimate(flops=flops, bytes_accessed=size, transcendentals=0),
        compiler_params=pltpu.CompilerParams(vmem_limit_bytes=32 * 2**20),
        name=name,
    )(*args)


def pack_kernel(dest_ref, x_ref, out_ref):
    for q in range(REQ_DEV):
        out_ref[dest_ref[q]] = x_ref[q]


def mix_kernel(
    source_ref, got_ref, last_ref, shift_ref, blend_ref, proj_ref, value_ref, decay_ref, learn_ref,
    out_ref, new_shift_ref, tokens,
):
    for page in range(REQ_DEV):
        tile = got_ref[source_ref[page]].astype(F32)
        for part in range(4):
            tokens[part, pl.ds(page, TS, stride=REQ_DEV), :] = tile[part * TS:(part + 1) * TS]
    current = jnp.concatenate([tokens[part] for part in range(4)], axis=1)
    before = jnp.concatenate([shift_ref[...], current[:-REQ_DEV]], axis=0)
    towards = before - current
    mixed = [(current + towards * blend_ref[b:b + 1, :]).astype(BF16) for b in range(5)]
    recept = dot(mixed[0], proj_ref[0]).astype(BF16)
    key = dot(mixed[2], proj_ref[1]).astype(BF16)
    value = dot(mixed[3], value_ref[...]).astype(BF16)
    decay = dot(mixed[1], decay_ref[...]).astype(BF16)
    learn = dot(mixed[4], learn_ref[...]).astype(BF16)
    pad = jnp.zeros((TOK, LANES - decay.shape[1]), BF16)
    for part in range(4):
        out_ref[part, :, 0:FEATS] = recept
        out_ref[part, :, FEATS:2 * FEATS] = key
        out_ref[part, :, 2 * FEATS:DECAY_AT] = value[:, part * VALS:(part + 1) * VALS]
        out_ref[part, :, DECAY_AT:LEARN_AT] = jnp.concatenate([decay, pad], axis=1)
        out_ref[part, :, LEARN_AT:WIDTH] = jnp.concatenate([learn, pad], axis=1)
    kept = last_ref[...]
    picked = current * jnp.concatenate([kept] * 4, axis=1)
    total = picked[0:REQ_DEV]
    for t in range(1, TS):
        total = total + picked[t * REQ_DEV:(t + 1) * REQ_DEV]
    new_shift_ref[...] = total


def state_kernel(
    got_ref, live_ref, state_ref, decay_ref, decay_offset_ref, learn_ref, learn_offset_ref, gain_ref,
    correction_ref, reward_ref, halves_ref, same_head_ref, head_to_lanes_ref,
    new_state_ref, reading_ref, bonus_ref, stat_ref, spread, states,
):
    total = got_ref[0].astype(F32)
    for part in range(1, 4):
        total = total + got_ref[part].astype(F32)
    recept = total[:, 0:FEATS]
    key = total[:, FEATS:2 * FEATS]
    value = total[:, 2 * FEATS:DECAY_AT]
    rank = decay_ref.shape[0]
    decay_low = jnp.tanh(total[:, DECAY_AT:DECAY_AT + rank]).astype(BF16)
    learn_low = total[:, LEARN_AT:LEARN_AT + learn_ref.shape[0]].astype(BF16)
    decay_in = decay_offset_ref[...] + dot(decay_low, decay_ref[...])
    learn = jax.nn.sigmoid(learn_offset_ref[...] + dot(learn_low, learn_ref[...]))
    decay = jnp.exp(jax.nn.sigmoid(decay_in) * (-float(np.exp(-0.5))))
    halves = halves_ref[...]
    scaled = key * gain_ref[...]
    squares = scaled * scaled
    norm = jnp.concatenate(
        [dot_split(squares[:, 0:256], halves), dot_split(squares[:, 256:512], halves)], axis=1
    )
    key_dir = scaled * lax.rsqrt(norm + 1e-6)
    key_adj = key * (1.0 + (learn - 1.0) * correction_ref[...])
    live = live_ref[...]
    live_wide = jnp.concatenate([live] * 4, axis=1)
    reward = dot_split(recept * key_adj * reward_ref[...], head_to_lanes_ref[...])
    bonus_ref[...] = reward * value * live
    vectors = [
        key_dir,
        jnp.where(live_wide > 0, decay, 1.0),
        key_dir * learn * live_wide,
        key_adj * live_wide,
        recept * live_wide,
    ]
    low_half = lax.broadcasted_iota(jnp.int32, (TOK, LANES), 1) < 64
    for at, vector in enumerate(vectors):
        for pair in range(HEADS // 2):
            block = vector[:, pair * LANES:(pair + 1) * LANES]
            turned = pltpu.roll(block, 64, 1)
            spread[at, 2 * pair] = jnp.where(low_half, block, turned)
            spread[at, 2 * pair + 1] = jnp.where(low_half, turned, block)
    lane = lax.broadcasted_iota(jnp.int32, (REQ_DEV, 256), 1)
    lane_key = lane % 64 - lane // 128
    value_pair = jnp.concatenate([value, value], axis=1)
    for head in range(HEADS):
        for quad in range(4):
            at = (head * 4 + quad) * REQ_DEV
            for half in range(2):
                for group in range(2):
                    start = group * 512 + (quad * 2 + half) * 8 + head
                    states[at + group * 8:at + group * 8 + 8, half * LANES:(half + 1) * LANES] = (
                        state_ref[pl.ds(start, 8, stride=64), :]
                    )
    for t in range(TS):
        rows = slice(t * REQ_DEV, (t + 1) * REQ_DEV)
        value_now = value_pair[rows]
        reading = jnp.zeros((REQ_DEV, LANES), F32)
        for head in range(HEADS):
            direction, keep, remove, add, query = [
                jnp.concatenate([jnp.concatenate([spread[at, head, rows, :]] * 2, axis=1)] * 4, axis=0)
                for at in range(5)
            ]
            masks = [lane_key == head * 8 + 2 * quad for quad in range(4)]
            place = slice(head * 64, (head + 1) * 64)
            state = states[place, :]
            removed = dot((state * direction).astype(BF16), halves)
            values = jnp.concatenate([jnp.where(m, value_now, 0.0) for m in masks], axis=0)
            spread_value = dot(values.astype(BF16), halves)
            state = state * keep - removed * remove + spread_value * add
            if t < TS - 1:
                states[place, :] = state
            else:
                for quad in range(4):
                    for half in range(2):
                        for group in range(2):
                            at = quad * REQ_DEV + group * 8
                            start = group * 512 + (quad * 2 + half) * 8 + head
                            new_state_ref[pl.ds(start, 8, stride=64), :] = state[
                                at:at + 8, half * LANES:(half + 1) * LANES
                            ]
            read = dot((state * query).astype(BF16), halves)
            for quad in range(4):
                part = jnp.where(masks[quad], read[quad * REQ_DEV:(quad + 1) * REQ_DEV], 0.0)
                reading = reading + part[:, 0:LANES] + part[:, LANES:256]
        reading_ref[rows, :] = reading
    reading = reading_ref[...]
    same_head = same_head_ref[...]
    head_sum = dot_split(reading, same_head)
    away = reading - head_sum * (1.0 / ROWS)
    away_sum = dot_split(away * away, same_head)
    stat = jnp.where(low_half, head_sum, away_sum)
    for part in range(4):
        stat_ref[part] = stat


def norm_kernel(source_ref, stat_ref, reading_ref, bonus_ref, gain_ref, to_natural_ref, out_ref, rows):
    low_half = lax.broadcasted_iota(jnp.int32, (TOK, LANES), 1) < 64
    sums, squares = [], []
    for part in range(4):
        stat = stat_ref[part]
        turned = pltpu.roll(stat, 64, 1)
        sums.append(jnp.where(low_half, stat, turned))
        squares.append(jnp.where(low_half, turned, stat))
    mean = (sums[0] + sums[1] + sums[2] + sums[3]) * (1.0 / CHANNEL_SPAN)
    spread = squares[0] + squares[1] + squares[2] + squares[3]
    for part in range(4):
        gap = sums[part] * (1.0 / ROWS) - mean
        spread = spread + gap * gap * float(ROWS)
    scale = lax.rsqrt(spread * (1.0 / CHANNEL_SPAN) + 0.00064)
    normed = (reading_ref[...] - mean) * scale * gain_ref[...] + bonus_ref[...]
    rows[...] = dot(normed.astype(BF16), to_natural_ref[...])
    for page in range(REQ_DEV):
        out_ref[source_ref[page]] = rows[pl.ds(page, TS, stride=REQ_DEV), :].astype(BF16)


def output_kernel(dest_ref, got_ref, proj_ref, out_ref, rows):
    for q in range(REQ_DEV):
        rows[q * TS:(q + 1) * TS, :] = got_ref[dest_ref[q]].astype(F32)
    terms = dot(rows[...].astype(BF16), proj_ref[...]).astype(BF16)
    for head in range(4):
        for part in range(4):
            out_ref[head * 4 + part] = terms[
                head * REQ_DEV:(head + 1) * REQ_DEV, part * FEATS:(part + 1) * FEATS
            ]


def shaped(shape, dtype):
    return jax.ShapeDtypeStruct(shape, dtype)


def per_device(
    incoming_activations,
    genuine_symbol_number,
    caller_sheet_slot,
    memory_sheets,
    prior_activation_sheets,
    blend_fractions,
    first_projectors,
    fading_narrow_projector,
    fading_widen_projector,
    fading_offset,
    context_step_narrowing,
    context_step_widening,
    context_step_offset,
    erasure_address_gain,
    address_correction,
    reward_coefficients,
    groupwise_gain,
    final_projector,
):
    groups = lax.axis_size("req")
    halves, same_head, head_to_lanes, to_natural, spread_values = [
        jnp.asarray(m, BF16) for m in constant_matrices()
    ]
    first = lax.axis_index("req") * REQ_DEV
    dest = lax.dynamic_slice_in_dim(caller_sheet_slot, first, REQ_DEV) // REQ_DEV
    pages = first + jnp.arange(REQ_DEV, dtype=jnp.int32)
    holder = caller_sheet_slot[None, :] == pages[:, None]
    everyone = jnp.arange(caller_sheet_slot.shape[0], dtype=jnp.int32)
    source = jnp.sum(jnp.where(holder, everyone[None, :], 0), axis=1) // REQ_DEV
    count = jnp.sum(jnp.where(holder, genuine_symbol_number[None, :], 0), axis=1)
    position = jnp.arange(TS, dtype=jnp.int32)[:, None]
    live = jnp.broadcast_to((position < count[None, :]).astype(F32)[..., None], (TS, REQ_DEV, LANES))
    last = jnp.broadcast_to(
        (position == count[None, :] - 1).astype(F32)[..., None], (TS, REQ_DEV, LANES)
    )
    live, last = live.reshape(TOK, LANES), last.reshape(TOK, LANES)

    tiles = incoming_activations.reshape(4, TS, 4, LANES).transpose(0, 2, 1, 3).reshape(4, 16, LANES)
    everywhere = jnp.broadcast_to(tiles[None], (4, 4, 16, LANES))
    mine = lax.all_to_all(everywhere, "head", 0, 0, tiled=True).reshape(REQ_DEV, 16, LANES)
    packed = call(
        pack_kernel, [shaped((groups, 16, LANES), BF16)], [SMEM, VMEM], (dest, mine), name="pack"
    )
    got = lax.all_to_all(packed, "req", 0, 0, tiled=True)
    value_projector = dot(first_projectors[2], spread_values).astype(BF16)
    partial, new_shift = call(
        mix_kernel,
        [shaped((4, TOK, WIDTH), BF16), shaped((REQ_DEV, FEATS), F32)],
        [SMEM] + [VMEM] * 8,
        (
            source, got, last, prior_activation_sheets, blend_fractions, first_projectors[0:2],
            value_projector, fading_narrow_projector, context_step_narrowing,
        ),
        scratch=[pltpu.VMEM((4, TOK, LANES), F32)],
        flops=2 * TOK * FEATS * (3 * FEATS + 192),
        name="mix",
    )
    sheets = memory_sheets.reshape(REQ_DEV, HEADS, 8, LANES).transpose(0, 2, 1, 3)
    sheets = sheets.reshape(REQ_DEV * HEADS * 8, LANES)
    sums = lax.all_to_all(partial, "row", 0, 0, tiled=True)
    new_state, reading, bonus, stat = call(
        state_kernel,
        [
            shaped((REQ_DEV * HEADS * 8, LANES), F32),
            shaped((TOK, LANES), F32),
            shaped((TOK, LANES), F32),
            shaped((4, TOK, LANES), F32),
        ],
        [VMEM] * 13,
        (
            sums,
            live,
            sheets,
            fading_widen_projector,
            fading_offset[None],
            context_step_widening,
            context_step_offset[None],
            erasure_address_gain[None],
            address_correction[None],
            reward_coefficients.reshape(1, FEATS),
            halves,
            same_head,
            head_to_lanes,
        ),
        scratch=[pltpu.VMEM((5, HEADS, TOK, LANES), F32), pltpu.VMEM((512, 256), F32)],
        flops=2 * 3 * TS * 512 * 256 * 256,
        name="state",
    )
    stats = lax.all_to_all(stat, "row", 0, 0, tiled=True)
    gain = groupwise_gain.reshape(HEADS, 8, 2).transpose(2, 0, 1).reshape(1, VALS)
    leaving = call(
        norm_kernel,
        [shaped((groups, TS, LANES), BF16)],
        [SMEM] + [VMEM] * 5,
        (source, stats, reading, bonus, gain, to_natural),
        scratch=[pltpu.VMEM((TOK, LANES), F32)],
        name="norm",
    )
    back = lax.all_to_all(leaving, "req", 0, 0, tiled=True)
    terms = call(
        output_kernel,
        [shaped((16, 16, FEATS), BF16)],
        [SMEM, VMEM, VMEM],
        (dest, back, final_projector.reshape(VALS, 4 * FEATS)),
        scratch=[pltpu.VMEM((TOK, LANES), F32)],
        flops=2 * TOK * VALS * 4 * FEATS,
        name="output",
    )
    arrived = lax.all_to_all(terms, ("head", "row"), 0, 0, tiled=True)
    mixed = jnp.sum(arrived.astype(F32), axis=0).astype(BF16).reshape(4, TS, FEATS)
    new_state = new_state.reshape(REQ_DEV, 8, HEADS, LANES).transpose(0, 2, 1, 3)
    return (mixed, new_state.reshape(REQ_DEV, HEADS, 8 * LANES), new_shift)


def solution(mesh):
    placed = (
        P(("req", "head"), None, "row"),
        P(),
        P(),
        P("req", "head", "row"),
        P("req", "row"),
        P(None, "row"),
        P(None, "row", "head"),
        P("row", None),
        P(None, "head"),
        P("head"),
        P("row", None),
        P(None, "head"),
        P("head"),
        P("head"),
        P("head"),
        P("head", None),
        P("head", "row"),
        P("head", "row", None),
    )
    return jax.shard_map(
        per_device,
        mesh=mesh,
        in_specs=placed,
        out_specs=(P(("req", "head"), None, "row"), P("req", "head", "row"), P("req", "row")),
        check_vma=False,
    )
```

```python
import functools

import jax
import jax.numpy as jnp
import numpy as np
from jax import lax
from jax.experimental import pallas as pl
from jax.experimental.pallas import tpu as pltpu
from jax.sharding import PartitionSpec as P

CHANNEL_SPAN = 64
TS = 4
REQ_DEV = 16
HEADS = 8
ROWS = 16
FEATS = HEADS * CHANNEL_SPAN
VALS = HEADS * ROWS
TOK = REQ_DEV * TS
LANES = 128
DECAY_AT = 2 * FEATS + VALS
LEARN_AT = DECAY_AT + LANES
WIDTH = LEARN_AT + LANES
F32 = jnp.float32
BF16 = jnp.bfloat16
VMEM = pl.BlockSpec(memory_space=pltpu.VMEM)
SMEM = pl.BlockSpec(memory_space=pltpu.SMEM)
ANY = pl.BlockSpec(memory_space=pl.ANY)


def value_lane(head, row):
    return (row % 2) * 64 + head * 8 + row // 2


def constant_matrices():
    lanes = np.arange(256)
    halves = (lanes[:, None] // 64 == lanes[None, :] // 64).astype(np.float32)
    c = np.arange(VALS)
    lane_head = (c % 64) // 8
    same_head = (lane_head[:, None] == lane_head[None, :]).astype(np.float32)
    head_to_lanes = (np.arange(FEATS)[:, None] // 64 == lane_head[None, :]).astype(np.float32)
    to_natural = np.zeros((VALS, VALS), np.float32)
    spread_values = np.zeros((FEATS, FEATS), np.float32)
    for head in range(HEADS):
        for row in range(ROWS):
            to_natural[value_lane(head, row), head * ROWS + row] = 1
            for part in range(4):
                spread_values[head * 64 + part * ROWS + row, part * VALS + value_lane(head, row)] = 1
    unpack = np.zeros((LANES, 2, LANES), np.float32)
    for side in range(2):
        unpack[side * 64:(side + 1) * 64, side] = same_head[side * 64:(side + 1) * 64]
    return halves, same_head, head_to_lanes, to_natural, spread_values, unpack.reshape(LANES, 256)


def dot(a, b):
    return jnp.dot(a, b, preferred_element_type=F32)


def dot_split(a, b):
    high = a.astype(BF16)
    low = (a - high.astype(F32)).astype(BF16)
    return dot(high, b) + dot(low, b)


def call(kernel, outs, in_specs, args, scratch=(), flops=0, name=None, out_spec=VMEM):
    size = sum(int(np.prod(a.shape)) * a.dtype.itemsize for a in args)
    size += sum(int(np.prod(o.shape)) * o.dtype.itemsize for o in outs)
    single = len(outs) == 1
    return pl.pallas_call(
        kernel,
        out_shape=outs[0] if single else outs,
        in_specs=in_specs,
        out_specs=out_spec if single else [out_spec] * len(outs),
        scratch_shapes=list(scratch),
        cost_estimate=pl.CostEstimate(flops=flops, bytes_accessed=size, transcendentals=0),
        compiler_params=pltpu.CompilerParams(vmem_limit_bytes=32 * 2**20),
        name=name,
    )(*args)


def fan_kernel(x_ref, out_ref, done):
    copies = [pltpu.make_async_copy(x_ref, out_ref.at[at], done.at[at]) for at in range(4)]
    for copy in copies:
        copy.start()
    for copy in copies:
        copy.wait()


def pack_kernel(dest_ref, x_ref, out_ref, done):
    copies = [
        pltpu.make_async_copy(x_ref.at[q], out_ref.at[dest_ref[q]], done.at[q])
        for q in range(REQ_DEV)
    ]
    for copy in copies:
        copy.start()
    for copy in copies:
        copy.wait()


def mix_kernel(
    source_ref, got_ref, last_ref, shift_ref, blend_ref, proj_ref, value_ref, decay_ref, learn_ref,
    out_ref, new_shift_ref, tokens,
):
    for page in range(REQ_DEV):
        tile = got_ref[source_ref[page]].astype(F32)
        for part in range(4):
            tokens[part, pl.ds(page, TS, stride=REQ_DEV), :] = tile[part * TS:(part + 1) * TS]
    current = jnp.concatenate([tokens[part] for part in range(4)], axis=1)
    before = jnp.concatenate([shift_ref[...], current[:-REQ_DEV]], axis=0)
    towards = before - current
    mixed = [(current + towards * blend_ref[b:b + 1, :]).astype(BF16) for b in range(5)]
    recept = dot(mixed[0], proj_ref[0]).astype(BF16)
    key = dot(mixed[2], proj_ref[1]).astype(BF16)
    value = dot(mixed[3], value_ref[...]).astype(BF16)
    decay = dot(mixed[1], decay_ref[...]).astype(BF16)
    learn = dot(mixed[4], learn_ref[...]).astype(BF16)
    pad = jnp.zeros((TOK, LANES - decay.shape[1]), BF16)
    for part in range(4):
        out_ref[part, :, 0:FEATS] = recept
        out_ref[part, :, FEATS:2 * FEATS] = key
        out_ref[part, :, 2 * FEATS:DECAY_AT] = value[:, part * VALS:(part + 1) * VALS]
        out_ref[part, :, DECAY_AT:LEARN_AT] = jnp.concatenate([decay, pad], axis=1)
        out_ref[part, :, LEARN_AT:WIDTH] = jnp.concatenate([learn, pad], axis=1)
    kept = last_ref[...]
    picked = current * jnp.concatenate([kept] * 4, axis=1)
    total = picked[0:REQ_DEV]
    for t in range(1, TS):
        total = total + picked[t * REQ_DEV:(t + 1) * REQ_DEV]
    new_shift_ref[...] = total


def state_kernel(
    got_ref, live_ref, state_ref, decay_ref, decay_offset_ref, learn_ref, learn_offset_ref, gain_ref,
    correction_ref, reward_ref, halves_ref, same_head_ref, head_to_lanes_ref,
    new_state_ref, reading_ref, bonus_ref, stat_ref, spread, states, factors,
):
    lane = lax.broadcasted_iota(jnp.int32, (REQ_DEV, 256), 1)
    lane_key = lane % 64 - lane // 128
    for head in range(HEADS):
        for quad in range(4):
            at = (head * 4 + quad) * REQ_DEV
            for half in range(2):
                for group in range(2):
                    start = group * 512 + (quad * 2 + half) * 8 + head
                    states[at + group * 8:at + group * 8 + 8, half * LANES:(half + 1) * LANES] = (
                        state_ref[pl.ds(start, 8, stride=64), :]
                    )
    total = got_ref[0].astype(F32)
    for part in range(1, 4):
        total = total + got_ref[part].astype(F32)
    recept = total[:, 0:FEATS]
    key = total[:, FEATS:2 * FEATS]
    value = total[:, 2 * FEATS:DECAY_AT]
    decay_low = jnp.tanh(total[:, DECAY_AT:DECAY_AT + decay_ref.shape[0]]).astype(BF16)
    learn_low = total[:, LEARN_AT:LEARN_AT + learn_ref.shape[0]].astype(BF16)
    decay_in = decay_offset_ref[...] + dot(decay_low, decay_ref[...])
    learn = jax.nn.sigmoid(learn_offset_ref[...] + dot(learn_low, learn_ref[...]))
    decay = jnp.exp(jax.nn.sigmoid(decay_in) * (-float(np.exp(-0.5))))
    halves = halves_ref[...]
    scaled = key * gain_ref[...]
    squares = scaled * scaled
    norm = dot_split(jnp.concatenate([squares[:, 0:256], squares[:, 256:512]], axis=0), halves)
    norm = jnp.concatenate([norm[0:TOK], norm[TOK:2 * TOK]], axis=1)
    key_dir = scaled * lax.rsqrt(norm + 1e-6)
    key_adj = key * (1.0 + (learn - 1.0) * correction_ref[...])
    live = live_ref[...]
    live_wide = jnp.concatenate([live] * 4, axis=1)
    vectors = [
        key_dir,
        jnp.where(live_wide > 0, decay, 1.0),
        key_dir * learn * live_wide,
        key_adj * live_wide,
        recept * live_wide,
    ]
    low_half = lax.broadcasted_iota(jnp.int32, (TOK, LANES), 1) < 64
    for at, vector in enumerate(vectors):
        for pair in range(HEADS // 2):
            block = vector[:, pair * LANES:(pair + 1) * LANES]
            turned = pltpu.roll(block, 64, 1)
            spread[at, 2 * pair] = jnp.where(low_half, block, turned)
            spread[at, 2 * pair + 1] = jnp.where(low_half, turned, block)
    value_pair = jnp.concatenate([value, value], axis=1)
    masks = [[lane_key == head * 8 + 2 * quad for quad in range(4)] for head in range(HEADS)]

    def vector_at(at, head, t):
        row = spread[at, head, t * REQ_DEV:(t + 1) * REQ_DEV, :]
        return jnp.concatenate([jnp.concatenate([row, row], axis=1)] * 4, axis=0)

    for t in range(TS + 1):
        for head in range(HEADS):
            place = slice(head * 64, (head + 1) * 64)
            state = states[place, :]
            if t > 0:
                removed = product[head * 64:(head + 1) * 64]
                added = product[512 + head * 64:512 + (head + 1) * 64]
                state = (
                    state * vector_at(1, head, t - 1)
                    - removed * vector_at(2, head, t - 1)
                    + added * vector_at(3, head, t - 1)
                )
                if t < TS:
                    states[place, :] = state
                else:
                    for quad in range(4):
                        for half in range(2):
                            for group in range(2):
                                at = quad * REQ_DEV + group * 8
                                start = group * 512 + (quad * 2 + half) * 8 + head
                                new_state_ref[pl.ds(start, 8, stride=64), :] = state[
                                    at:at + 8, half * LANES:(half + 1) * LANES
                                ]
                query = (state * vector_at(4, head, t - 1)).astype(BF16)
                factors[1024 + head * 64:1024 + (head + 1) * 64, :] = query
            if t < TS:
                factors[place, :] = (state * vector_at(0, head, t)).astype(BF16)
                now = value_pair[t * REQ_DEV:(t + 1) * REQ_DEV]
                picked = jnp.concatenate([jnp.where(m, now, 0.0) for m in masks[head]], axis=0)
                factors[512 + head * 64:512 + (head + 1) * 64, :] = picked.astype(BF16)
        first = 0 if t < TS else 1024
        last = 1536 if t > 0 else 1024
        product = dot(factors[first:last, :], halves)
        if t > 0:
            read = product[1024 - first:]
            reading = jnp.zeros((REQ_DEV, LANES), F32)
            for head in range(HEADS):
                for quad in range(4):
                    at = (head * 4 + quad) * REQ_DEV
                    part = jnp.where(masks[head][quad], read[at:at + REQ_DEV], 0.0)
                    reading = reading + part[:, 0:LANES] + part[:, LANES:256]
            reading_ref[(t - 1) * REQ_DEV:t * REQ_DEV, :] = reading
    reward = dot_split(recept * key_adj * reward_ref[...], head_to_lanes_ref[...])
    bonus_ref[...] = reward * value * live
    reading = reading_ref[...]
    same_head = same_head_ref[...]
    head_sum = dot_split(reading, same_head)
    away = reading - head_sum * (1.0 / ROWS)
    away_sum = dot_split(away * away, same_head)
    stat = jnp.where(low_half, head_sum, away_sum)
    slot = lax.broadcasted_iota(jnp.int32, (8, LANES), 1) % 8
    packed = jnp.zeros((8, LANES), F32)
    for group in range(8):
        packed = packed + jnp.where(slot == group, stat[group * 8:(group + 1) * 8], 0.0)
    for part in range(4):
        stat_ref[part] = packed


def norm_kernel(source_ref, stat_ref, reading_ref, bonus_ref, gain_ref, unpack_ref, to_natural_ref, out_ref, rows):
    lane = lax.broadcasted_iota(jnp.int32, (8, LANES), 1)
    stats = [stat_ref[part] for part in range(4)]
    mean = (stats[0] + stats[1] + stats[2] + stats[3]) * (1.0 / CHANNEL_SPAN)
    away = pltpu.roll(stats[0] + stats[1] + stats[2] + stats[3], 64, 1)
    for part in range(4):
        gap = stats[part] * (1.0 / ROWS) - mean
        away = away + gap * gap * float(ROWS)
    scale = lax.rsqrt(jnp.where(lane < 64, away, 0.0) * (1.0 / CHANNEL_SPAN) + 0.00064)
    both = jnp.where(lane < 64, mean, pltpu.roll(scale, 64, 1))
    packed = jnp.concatenate([jnp.where(lane % 8 == group, both, 0.0) for group in range(8)], axis=0)
    high = packed.astype(BF16)
    rest = packed - high.astype(F32)
    middle = rest.astype(BF16)
    low = (rest - middle.astype(F32)).astype(BF16)
    opened = dot(jnp.concatenate([high, middle, low], axis=0), unpack_ref[...])
    opened = opened[0:TOK] + opened[TOK:2 * TOK] + opened[2 * TOK:3 * TOK]
    normed = (reading_ref[...] - opened[:, 0:LANES]) * opened[:, LANES:256] * gain_ref[...] + bonus_ref[...]
    rows[...] = dot(normed.astype(BF16), to_natural_ref[...])
    for page in range(REQ_DEV):
        out_ref[source_ref[page]] = rows[pl.ds(page, TS, stride=REQ_DEV), :].astype(BF16)


def output_kernel(dest_ref, got_ref, proj_ref, out_ref, rows):
    for q in range(REQ_DEV):
        rows[q * TS:(q + 1) * TS, :] = got_ref[dest_ref[q]].astype(F32)
    terms = dot(rows[...].astype(BF16), proj_ref[...]).astype(BF16)
    for head in range(4):
        for part in range(4):
            out_ref[head * 4 + part] = terms[
                head * REQ_DEV:(head + 1) * REQ_DEV, part * FEATS:(part + 1) * FEATS
            ]


def shaped(shape, dtype):
    return jax.ShapeDtypeStruct(shape, dtype)


def per_device(
    incoming_activations,
    genuine_symbol_number,
    caller_sheet_slot,
    memory_sheets,
    prior_activation_sheets,
    blend_fractions,
    first_projectors,
    fading_narrow_projector,
    fading_widen_projector,
    fading_offset,
    context_step_narrowing,
    context_step_widening,
    context_step_offset,
    erasure_address_gain,
    address_correction,
    reward_coefficients,
    groupwise_gain,
    final_projector,
):
    groups = lax.axis_size("req")
    halves, same_head, head_to_lanes, to_natural, spread_values, unpack = [
        jnp.asarray(m, BF16) for m in constant_matrices()
    ]
    first = lax.axis_index("req") * REQ_DEV
    dest = lax.dynamic_slice_in_dim(caller_sheet_slot, first, REQ_DEV) // REQ_DEV
    pages = first + jnp.arange(REQ_DEV, dtype=jnp.int32)
    holder = caller_sheet_slot[None, :] == pages[:, None]
    everyone = jnp.arange(caller_sheet_slot.shape[0], dtype=jnp.int32)
    source = jnp.sum(jnp.where(holder, everyone[None, :], 0), axis=1) // REQ_DEV
    count = jnp.sum(jnp.where(holder, genuine_symbol_number[None, :], 0), axis=1)
    position = jnp.arange(TS, dtype=jnp.int32)[:, None]
    live = jnp.broadcast_to((position < count[None, :]).astype(F32)[..., None], (TS, REQ_DEV, LANES))
    last = jnp.broadcast_to(
        (position == count[None, :] - 1).astype(F32)[..., None], (TS, REQ_DEV, LANES)
    )
    live, last = live.reshape(TOK, LANES), last.reshape(TOK, LANES)

    tiles = incoming_activations.reshape(4, TS, 4, LANES).transpose(0, 2, 1, 3).reshape(4, 16, LANES)
    everywhere = call(
        fan_kernel,
        [shaped((4, 4, 16, LANES), BF16)],
        [ANY],
        (tiles,),
        scratch=[pltpu.SemaphoreType.DMA((4,))],
        name="fan",
        out_spec=ANY,
    )
    mine = lax.all_to_all(everywhere, "head", 0, 0, tiled=True).reshape(REQ_DEV, 16, LANES)
    packed = call(
        pack_kernel,
        [shaped((groups, 16, LANES), BF16)],
        [SMEM, ANY],
        (dest, mine),
        scratch=[pltpu.SemaphoreType.DMA((REQ_DEV,))],
        name="pack",
        out_spec=ANY,
    )
    got = lax.all_to_all(packed, "req", 0, 0, tiled=True)
    value_projector = dot(first_projectors[2], spread_values).astype(BF16)
    partial, new_shift = call(
        mix_kernel,
        [shaped((4, TOK, WIDTH), BF16), shaped((REQ_DEV, FEATS), F32)],
        [SMEM] + [VMEM] * 8,
        (
            source, got, last, prior_activation_sheets, blend_fractions, first_projectors[0:2],
            value_projector, fading_narrow_projector, context_step_narrowing,
        ),
        scratch=[pltpu.VMEM((4, TOK, LANES), F32)],
        flops=2 * TOK * FEATS * (3 * FEATS + 192),
        name="mix",
    )
    sheets = memory_sheets.reshape(REQ_DEV, HEADS, 8, LANES).transpose(0, 2, 1, 3)
    sheets = sheets.reshape(REQ_DEV * HEADS * 8, LANES)
    sums = lax.all_to_all(partial, "row", 0, 0, tiled=True)
    new_state, reading, bonus, stat = call(
        state_kernel,
        [
            shaped((REQ_DEV * HEADS * 8, LANES), F32),
            shaped((TOK, LANES), F32),
            shaped((TOK, LANES), F32),
            shaped((4, 8, LANES), F32),
        ],
        [VMEM] * 13,
        (
            sums,
            live,
            sheets,
            fading_widen_projector,
            fading_offset[None],
            context_step_widening,
            context_step_offset[None],
            erasure_address_gain[None],
            address_correction[None],
            reward_coefficients.reshape(1, FEATS),
            halves,
            same_head,
            head_to_lanes,
        ),
        scratch=[pltpu.VMEM((5, HEADS, TOK, LANES), F32), pltpu.VMEM((512, 256), F32), pltpu.VMEM((1536, 256), BF16)],
        flops=2 * 3 * TS * 512 * 256 * 256,
        name="state",
    )
    stats = lax.all_to_all(stat, "row", 0, 0, tiled=True)
    gain = groupwise_gain.reshape(HEADS, 8, 2).transpose(2, 0, 1).reshape(1, VALS)
    leaving = call(
        norm_kernel,
        [shaped((groups, TS, LANES), BF16)],
        [SMEM] + [VMEM] * 6,
        (source, stats, reading, bonus, gain, unpack, to_natural),
        scratch=[pltpu.VMEM((TOK, LANES), F32)],
        name="norm",
    )
    back = lax.all_to_all(leaving, "req", 0, 0, tiled=True)
    terms = call(
        output_kernel,
        [shaped((16, 16, FEATS), BF16)],
        [SMEM, VMEM, VMEM],
        (dest, back, final_projector.reshape(VALS, 4 * FEATS)),
        scratch=[pltpu.VMEM((TOK, LANES), F32)],
        flops=2 * TOK * VALS * 4 * FEATS,
        name="output",
    )
    arrived = lax.all_to_all(terms, ("head", "row"), 0, 0, tiled=True)
    mixed = jnp.sum(arrived.astype(F32), axis=0).astype(BF16).reshape(4, TS, FEATS)
    new_state = new_state.reshape(REQ_DEV, 8, HEADS, LANES).transpose(0, 2, 1, 3)
    return (mixed, new_state.reshape(REQ_DEV, HEADS, 8 * LANES), new_shift)


def solution(mesh):
    placed = (
        P(("req", "head"), None, "row"),
        P(),
        P(),
        P("req", "head", "row"),
        P("req", "row"),
        P(None, "row"),
        P(None, "row", "head"),
        P("row", None),
        P(None, "head"),
        P("head"),
        P("row", None),
        P(None, "head"),
        P("head"),
        P("head"),
        P("head"),
        P("head", None),
        P("head", "row"),
        P("head", "row", None),
    )
    return jax.shard_map(
        per_device,
        mesh=mesh,
        in_specs=placed,
        out_specs=(P(("req", "head"), None, "row"), P("req", "head", "row"), P("req", "row")),
        check_vma=False,
    )
```

```python
import functools

import jax
import jax.numpy as jnp
import numpy as np
from jax import lax
from jax.experimental import pallas as pl
from jax.experimental.pallas import tpu as pltpu
from jax.sharding import PartitionSpec as P

CHANNEL_SPAN = 64
TS = 4
REQ_DEV = 16
HEADS = 8
ROWS = 16
FEATS = HEADS * CHANNEL_SPAN
VALS = HEADS * ROWS
TOK = REQ_DEV * TS
LANES = 128
DECAY_AT = 2 * FEATS + VALS
LEARN_AT = DECAY_AT + LANES
WIDTH = LEARN_AT + LANES
F32 = jnp.float32
BF16 = jnp.bfloat16
VMEM = pl.BlockSpec(memory_space=pltpu.VMEM)
SMEM = pl.BlockSpec(memory_space=pltpu.SMEM)
ANY = pl.BlockSpec(memory_space=pl.ANY)


def value_lane(head, row):
    return (row % 2) * 64 + head * 8 + row // 2


def constant_matrices():
    lanes = np.arange(256)
    halves = (lanes[:, None] // 64 == lanes[None, :] // 64).astype(np.float32)
    c = np.arange(VALS)
    lane_head = (c % 64) // 8
    same_head = (lane_head[:, None] == lane_head[None, :]).astype(np.float32)
    head_to_lanes = (np.arange(FEATS)[:, None] // 64 == lane_head[None, :]).astype(np.float32)
    to_natural = np.zeros((VALS, VALS), np.float32)
    spread_values = np.zeros((FEATS, FEATS), np.float32)
    for head in range(HEADS):
        for row in range(ROWS):
            to_natural[value_lane(head, row), head * ROWS + row] = 1
            for part in range(4):
                spread_values[head * 64 + part * ROWS + row, part * VALS + value_lane(head, row)] = 1
    unpack = np.zeros((LANES, 2, LANES), np.float32)
    for side in range(2):
        unpack[side * 64:(side + 1) * 64, side] = same_head[side * 64:(side + 1) * 64]
    return halves, same_head, head_to_lanes, to_natural, spread_values, unpack.reshape(LANES, 256)


def dot(a, b):
    return jnp.dot(a, b, preferred_element_type=F32)


def dot_split(a, b):
    high = a.astype(BF16)
    low = (a - high.astype(F32)).astype(BF16)
    return dot(high, b) + dot(low, b)


def call(kernel, outs, in_specs, args, scratch=(), flops=0, name=None, out_spec=VMEM):
    size = sum(int(np.prod(a.shape)) * a.dtype.itemsize for a in args)
    size += sum(int(np.prod(o.shape)) * o.dtype.itemsize for o in outs)
    single = len(outs) == 1
    return pl.pallas_call(
        kernel,
        out_shape=outs[0] if single else outs,
        in_specs=in_specs,
        out_specs=out_spec if single else [out_spec] * len(outs),
        scratch_shapes=list(scratch),
        cost_estimate=pl.CostEstimate(flops=flops, bytes_accessed=size, transcendentals=0),
        compiler_params=pltpu.CompilerParams(vmem_limit_bytes=32 * 2**20),
        name=name,
    )(*args)


def fan_kernel(x_ref, out_ref, done):
    copies = [pltpu.make_async_copy(x_ref, out_ref.at[at], done.at[at]) for at in range(4)]
    for copy in copies:
        copy.start()
    for copy in copies:
        copy.wait()


def pack_kernel(slot_ref, first_ref, x_ref, out_ref):
    for q in range(REQ_DEV):
        out_ref[slot_ref[first_ref[0] + q] // REQ_DEV] = x_ref[q]


def mix_kernel(
    source_ref, count_ref, got_ref, shift_ref, blend_ref, proj_ref, decay_ref, learn_ref, spread_ref,
    out_ref, new_shift_ref, tokens,
):
    for page in range(REQ_DEV):
        tile = got_ref[source_ref[page]].astype(F32)
        for part in range(4):
            tokens[part, pl.ds(page, TS, stride=REQ_DEV), :] = tile[part * TS:(part + 1) * TS]
    current = jnp.concatenate([tokens[part] for part in range(4)], axis=1)
    before = jnp.concatenate([shift_ref[...], current[:-REQ_DEV]], axis=0)
    towards = before - current

    def mixed(branch):
        return (current + towards * blend_ref[branch:branch + 1, :]).astype(BF16)

    def low_rank(rows, weight):
        return lax.dot_general(
            rows, weight, (((1,), (1,)), ((), ())), preferred_element_type=F32
        ).astype(BF16)

    value = dot(dot(mixed(3), proj_ref[2]).astype(BF16), spread_ref[...]).astype(BF16)
    recept = dot(mixed(0), proj_ref[0]).astype(BF16)
    key = dot(mixed(2), proj_ref[1]).astype(BF16)
    decay = low_rank(mixed(1), decay_ref[...])
    learn = low_rank(mixed(4), learn_ref[...])
    pad = jnp.zeros((TOK, LANES - decay.shape[1]), BF16)
    for part in range(4):
        out_ref[part, :, 0:FEATS] = recept
        out_ref[part, :, FEATS:2 * FEATS] = key
        out_ref[part, :, 2 * FEATS:DECAY_AT] = value[:, part * VALS:(part + 1) * VALS]
        out_ref[part, :, DECAY_AT:LEARN_AT] = jnp.concatenate([decay, pad], axis=1)
        out_ref[part, :, LEARN_AT:WIDTH] = jnp.concatenate([learn, pad], axis=1)
    for page in range(REQ_DEV):
        row = (count_ref[page] - 1) * REQ_DEV + page
        for part in range(4):
            new_shift_ref[page:page + 1, part * LANES:(part + 1) * LANES] = tokens[part, pl.ds(row, 1), :]


def state_kernel(
    count_ref, got_ref, state_ref, decay_ref, decay_offset_ref, learn_ref, learn_offset_ref, gain_ref,
    correction_ref, reward_ref, halves_ref, same_head_ref, head_to_lanes_ref,
    new_state_ref, reading_ref, bonus_ref, stat_ref, spread, states, factors,
):
    lane = lax.broadcasted_iota(jnp.int32, (REQ_DEV, 256), 1)
    lane_key = lane % 64 - lane // 128
    for head in range(HEADS):
        for quad in range(4):
            at = (head * 4 + quad) * REQ_DEV
            for half in range(2):
                for group in range(2):
                    start = group * 512 + (quad * 2 + half) * 8 + head
                    states[at + group * 8:at + group * 8 + 8, half * LANES:(half + 1) * LANES] = (
                        state_ref[pl.ds(start, 8, stride=64), :]
                    )
    total = got_ref[0].astype(F32)
    for part in range(1, 4):
        total = total + got_ref[part].astype(F32)
    recept = total[:, 0:FEATS]
    key = total[:, FEATS:2 * FEATS]
    value = total[:, 2 * FEATS:DECAY_AT]
    decay_low = jnp.tanh(total[:, DECAY_AT:DECAY_AT + decay_ref.shape[0]]).astype(BF16)
    learn_low = total[:, LEARN_AT:LEARN_AT + learn_ref.shape[0]].astype(BF16)
    decay_in = decay_offset_ref[...] + dot(decay_low, decay_ref[...])
    learn = jax.nn.sigmoid(learn_offset_ref[...] + dot(learn_low, learn_ref[...]))
    decay = jnp.exp(jax.nn.sigmoid(decay_in) * (-float(np.exp(-0.5))))
    halves = halves_ref[...]
    scaled = key * gain_ref[...]
    squares = scaled * scaled
    norm = dot_split(jnp.concatenate([squares[:, 0:256], squares[:, 256:512]], axis=0), halves)
    norm = jnp.concatenate([norm[0:TOK], norm[TOK:2 * TOK]], axis=1)
    key_dir = scaled * lax.rsqrt(norm + 1e-6)
    key_adj = key * (1.0 + (learn - 1.0) * correction_ref[...])
    page_row = lax.broadcasted_iota(jnp.int32, (REQ_DEV, LANES), 0)
    counts = jnp.zeros((REQ_DEV, LANES), jnp.int32)
    for page in range(REQ_DEV):
        counts = jnp.where(page_row == page, count_ref[page], counts)
    live = jnp.concatenate([jnp.where(counts > t, 1.0, 0.0) for t in range(TS)], axis=0)
    live_wide = jnp.concatenate([live] * 4, axis=1)
    vectors = [
        key_dir,
        jnp.where(live_wide > 0, decay, 1.0),
        key_dir * learn * live_wide,
        key_adj * live_wide,
        recept * live_wide,
    ]
    low_half = lax.broadcasted_iota(jnp.int32, (TOK, LANES), 1) < 64
    for at, vector in enumerate(vectors):
        for pair in range(HEADS // 2):
            block = vector[:, pair * LANES:(pair + 1) * LANES]
            turned = pltpu.roll(block, 64, 1)
            spread[at, 2 * pair] = jnp.where(low_half, block, turned)
            spread[at, 2 * pair + 1] = jnp.where(low_half, turned, block)
    value_pair = jnp.concatenate([value, value], axis=1)
    masks = [[lane_key == head * 8 + 2 * quad for quad in range(4)] for head in range(HEADS)]

    def vector_at(at, head, t):
        row = spread[at, head, t * REQ_DEV:(t + 1) * REQ_DEV, :]
        return jnp.concatenate([jnp.concatenate([row, row], axis=1)] * 4, axis=0)

    for t in range(TS + 1):
        for head in range(HEADS):
            place = slice(head * 64, (head + 1) * 64)
            state = states[place, :]
            if t > 0:
                removed = product[head * 64:(head + 1) * 64]
                added = product[512 + head * 64:512 + (head + 1) * 64]
                state = (
                    state * vector_at(1, head, t - 1)
                    - removed * vector_at(2, head, t - 1)
                    + added * vector_at(3, head, t - 1)
                )
                if t < TS:
                    states[place, :] = state
                else:
                    for quad in range(4):
                        for half in range(2):
                            for group in range(2):
                                at = quad * REQ_DEV + group * 8
                                start = group * 512 + (quad * 2 + half) * 8 + head
                                new_state_ref[pl.ds(start, 8, stride=64), :] = state[
                                    at:at + 8, half * LANES:(half + 1) * LANES
                                ]
                query = (state * vector_at(4, head, t - 1)).astype(BF16)
                factors[1024 + head * 64:1024 + (head + 1) * 64, :] = query
            if t < TS:
                factors[place, :] = (state * vector_at(0, head, t)).astype(BF16)
                now = value_pair[t * REQ_DEV:(t + 1) * REQ_DEV]
                picked = jnp.concatenate([jnp.where(m, now, 0.0) for m in masks[head]], axis=0)
                factors[512 + head * 64:512 + (head + 1) * 64, :] = picked.astype(BF16)
        first = 0 if t < TS else 1024
        last = 1536 if t > 0 else 1024
        product = dot(factors[first:last, :], halves)
        if t > 0:
            read = product[1024 - first:]
            reading = jnp.zeros((REQ_DEV, LANES), F32)
            for head in range(HEADS):
                for quad in range(4):
                    at = (head * 4 + quad) * REQ_DEV
                    part = jnp.where(masks[head][quad], read[at:at + REQ_DEV], 0.0)
                    reading = reading + part[:, 0:LANES] + part[:, LANES:256]
            reading_ref[(t - 1) * REQ_DEV:t * REQ_DEV, :] = reading
    reward = dot_split(recept * key_adj * reward_ref[...], head_to_lanes_ref[...])
    bonus_ref[...] = reward * value * live
    reading = reading_ref[...]
    same_head = same_head_ref[...]
    head_sum = dot_split(reading, same_head)
    away = reading - head_sum * (1.0 / ROWS)
    away_sum = dot_split(away * away, same_head)
    stat = jnp.where(low_half, head_sum, away_sum)
    slot = lax.broadcasted_iota(jnp.int32, (8, LANES), 1) % 8
    packed = jnp.zeros((8, LANES), F32)
    for group in range(8):
        packed = packed + jnp.where(slot == group, stat[group * 8:(group + 1) * 8], 0.0)
    for part in range(4):
        stat_ref[part] = packed


def norm_kernel(source_ref, stat_ref, reading_ref, bonus_ref, gain_ref, unpack_ref, to_natural_ref, out_ref, rows):
    lane = lax.broadcasted_iota(jnp.int32, (8, LANES), 1)
    stats = [stat_ref[part] for part in range(4)]
    mean = (stats[0] + stats[1] + stats[2] + stats[3]) * (1.0 / CHANNEL_SPAN)
    away = pltpu.roll(stats[0] + stats[1] + stats[2] + stats[3], 64, 1)
    for part in range(4):
        gap = stats[part] * (1.0 / ROWS) - mean
        away = away + gap * gap * float(ROWS)
    scale = lax.rsqrt(jnp.where(lane < 64, away, 0.0) * (1.0 / CHANNEL_SPAN) + 0.00064)
    both = jnp.where(lane < 64, mean, pltpu.roll(scale, 64, 1))
    packed = jnp.concatenate([jnp.where(lane % 8 == group, both, 0.0) for group in range(8)], axis=0)
    high = packed.astype(BF16)
    rest = packed - high.astype(F32)
    middle = rest.astype(BF16)
    low = (rest - middle.astype(F32)).astype(BF16)
    opened = dot(jnp.concatenate([high, middle, low], axis=0), unpack_ref[...])
    opened = opened[0:TOK] + opened[TOK:2 * TOK] + opened[2 * TOK:3 * TOK]
    normed = (reading_ref[...] - opened[:, 0:LANES]) * opened[:, LANES:256] * gain_ref[...] + bonus_ref[...]
    rows[...] = dot(normed.astype(BF16), to_natural_ref[...])
    for page in range(REQ_DEV):
        out_ref[source_ref[page]] = rows[pl.ds(page, TS, stride=REQ_DEV), :].astype(BF16)


def output_kernel(slot_ref, first_ref, got_ref, proj_ref, out_ref, rows):
    for q in range(REQ_DEV):
        rows[q * TS:(q + 1) * TS, :] = got_ref[slot_ref[first_ref[0] + q] // REQ_DEV].astype(F32)
    terms = dot(rows[...].astype(BF16), proj_ref[...]).astype(BF16)
    for head in range(4):
        for part in range(4):
            out_ref[head * 4 + part] = terms[
                head * REQ_DEV:(head + 1) * REQ_DEV, part * FEATS:(part + 1) * FEATS
            ]


def shaped(shape, dtype):
    return jax.ShapeDtypeStruct(shape, dtype)


def per_device(
    incoming_activations,
    genuine_symbol_number,
    caller_sheet_slot,
    memory_sheets,
    prior_activation_sheets,
    blend_fractions,
    first_projectors,
    fading_narrow_projector,
    fading_widen_projector,
    fading_offset,
    context_step_narrowing,
    context_step_widening,
    context_step_offset,
    erasure_address_gain,
    address_correction,
    reward_coefficients,
    groupwise_gain,
    final_projector,
):
    groups = lax.axis_size("req")
    halves, same_head, head_to_lanes, to_natural, spread_values, unpack = [
        jnp.asarray(m, BF16) for m in constant_matrices()
    ]
    first = lax.axis_index("req") * REQ_DEV
    pages = first + jnp.arange(REQ_DEV, dtype=jnp.int32)
    holder = caller_sheet_slot[None, :] == pages[:, None]
    groups_of = lax.shift_right_logical(jnp.arange(caller_sheet_slot.shape[0], dtype=jnp.int32), 4)
    source = jnp.sum(jnp.where(holder, groups_of[None, :], 0), axis=1)
    count = jnp.sum(jnp.where(holder, genuine_symbol_number[None, :], 0), axis=1)
    first = first.astype(jnp.int32)[None]
    gain = groupwise_gain.reshape(HEADS, 8, 2).transpose(2, 0, 1).reshape(1, VALS)
    reward = reward_coefficients.reshape(1, FEATS)

    tiles = incoming_activations.reshape(4, TS, 4, LANES).transpose(0, 2, 1, 3).reshape(4, 16, LANES)
    everywhere = call(
        fan_kernel,
        [shaped((4, 4, 16, LANES), BF16)],
        [pl.BlockSpec(memory_space=pltpu.HBM)],
        (tiles,),
        scratch=[pltpu.SemaphoreType.DMA((4,))],
        name="fan",
        out_spec=ANY,
    )
    mine = lax.all_to_all(everywhere, "head", 0, 0, tiled=True).reshape(REQ_DEV, 16, LANES)
    mine, source, count, gain, reward = lax.optimization_barrier((mine, source, count, gain, reward))
    packed = call(
        pack_kernel,
        [shaped((groups, 16, LANES), BF16)],
        [SMEM, SMEM, VMEM],
        (caller_sheet_slot, first, mine),
        name="pack",
    )
    got = lax.all_to_all(packed, "req", 0, 0, tiled=True)
    partial, new_shift = call(
        mix_kernel,
        [shaped((4, TOK, WIDTH), BF16), shaped((REQ_DEV, FEATS), F32)],
        [SMEM] * 2 + [VMEM] * 7,
        (
            source, count, got, prior_activation_sheets, blend_fractions, first_projectors,
            fading_narrow_projector.T, context_step_narrowing.T, spread_values,
        ),
        scratch=[pltpu.VMEM((4, TOK, LANES), F32)],
        flops=2 * TOK * FEATS * (3 * FEATS + 192),
        name="mix",
    )
    sheets = memory_sheets.reshape(REQ_DEV, HEADS, 8, LANES).transpose(0, 2, 1, 3)
    sheets = sheets.reshape(REQ_DEV * HEADS * 8, LANES)
    sums = lax.all_to_all(partial, "row", 0, 0, tiled=True)
    new_state, reading, bonus, stat = call(
        state_kernel,
        [
            shaped((REQ_DEV * HEADS * 8, LANES), F32),
            shaped((TOK, LANES), F32),
            shaped((TOK, LANES), F32),
            shaped((4, 8, LANES), F32),
        ],
        [SMEM] + [VMEM] * 12,
        (
            count,
            sums,
            sheets,
            fading_widen_projector,
            fading_offset[None],
            context_step_widening,
            context_step_offset[None],
            erasure_address_gain[None],
            address_correction[None],
            reward,
            halves,
            same_head,
            head_to_lanes,
        ),
        scratch=[pltpu.VMEM((5, HEADS, TOK, LANES), F32), pltpu.VMEM((512, 256), F32), pltpu.VMEM((1536, 256), BF16)],
        flops=2 * 3 * TS * 512 * 256 * 256,
        name="state",
    )
    stats = lax.all_to_all(stat, "row", 0, 0, tiled=True)
    leaving = call(
        norm_kernel,
        [shaped((groups, TS, LANES), BF16)],
        [SMEM] + [VMEM] * 6,
        (source, stats, reading, bonus, gain, unpack, to_natural),
        scratch=[pltpu.VMEM((TOK, LANES), F32)],
        name="norm",
    )
    back = lax.all_to_all(leaving, "req", 0, 0, tiled=True)
    terms = call(
        output_kernel,
        [shaped((16, 16, FEATS), BF16)],
        [SMEM, SMEM, VMEM, VMEM],
        (caller_sheet_slot, first, back, final_projector.reshape(VALS, 4 * FEATS)),
        scratch=[pltpu.VMEM((TOK, LANES), F32)],
        flops=2 * TOK * VALS * 4 * FEATS,
        name="output",
    )
    arrived = lax.all_to_all(terms, ("head", "row"), 0, 0, tiled=True)
    mixed = jnp.sum(arrived.astype(F32), axis=0).astype(BF16).reshape(4, TS, FEATS)
    new_state = new_state.reshape(REQ_DEV, 8, HEADS, LANES).transpose(0, 2, 1, 3)
    return (mixed, new_state.reshape(REQ_DEV, HEADS, 8 * LANES), new_shift)


def solution(mesh):
    placed = (
        P(("req", "head"), None, "row"),
        P(),
        P(),
        P("req", "head", "row"),
        P("req", "row"),
        P(None, "row"),
        P(None, "row", "head"),
        P("row", None),
        P(None, "head"),
        P("head"),
        P("row", None),
        P(None, "head"),
        P("head"),
        P("head"),
        P("head"),
        P("head", None),
        P("head", "row"),
        P("head", "row", None),
    )
    return jax.shard_map(
        per_device,
        mesh=mesh,
        in_specs=placed,
        out_specs=(P(("req", "head"), None, "row"), P("req", "head", "row"), P("req", "row")),
        check_vma=False,
    )
```

```python
import functools

import jax
import jax.numpy as jnp
import numpy as np
from jax import lax
from jax.experimental import pallas as pl
from jax.experimental.pallas import tpu as pltpu
from jax.sharding import PartitionSpec as P

CHANNEL_SPAN = 64
TS = 4
REQ_DEV = 16
HEADS = 8
ROWS = 16
FEATS = HEADS * CHANNEL_SPAN
VALS = HEADS * ROWS
TOK = REQ_DEV * TS
LANES = 128
DECAY_AT = 2 * FEATS + VALS
LEARN_AT = DECAY_AT + LANES
WIDTH = LEARN_AT + LANES
F32 = jnp.float32
BF16 = jnp.bfloat16
VMEM = pl.BlockSpec(memory_space=pltpu.VMEM)
SMEM = pl.BlockSpec(memory_space=pltpu.SMEM)
ANY = pl.BlockSpec(memory_space=pl.ANY)


def value_lane(head, row):
    return (row % 2) * 64 + head * 8 + row // 2


def constant_matrices():
    lanes = np.arange(256)
    halves = (lanes[:, None] // 64 == lanes[None, :] // 64).astype(np.float32)
    c = np.arange(VALS)
    lane_head = (c % 64) // 8
    same_head = (lane_head[:, None] == lane_head[None, :]).astype(np.float32)
    head_to_lanes = (np.arange(FEATS)[:, None] // 64 == lane_head[None, :]).astype(np.float32)
    to_natural = np.zeros((VALS, VALS), np.float32)
    spread_values = np.zeros((FEATS, FEATS), np.float32)
    for head in range(HEADS):
        for row in range(ROWS):
            to_natural[value_lane(head, row), head * ROWS + row] = 1
            for part in range(4):
                spread_values[head * 64 + part * ROWS + row, part * VALS + value_lane(head, row)] = 1
    unpack = np.zeros((LANES, 2, LANES), np.float32)
    for side in range(2):
        unpack[side * 64:(side + 1) * 64, side] = same_head[side * 64:(side + 1) * 64]
    return halves, same_head, head_to_lanes, to_natural, spread_values, unpack.reshape(LANES, 256)


def dot(a, b):
    return jnp.dot(a, b, preferred_element_type=F32)


def dot_split(a, b):
    high = a.astype(BF16)
    low = (a - high.astype(F32)).astype(BF16)
    return dot(high, b) + dot(low, b)


def call(kernel, outs, in_specs, args, scratch=(), flops=0, name=None, out_spec=VMEM, vmem=32 * 2**20):
    size = sum(int(np.prod(a.shape)) * a.dtype.itemsize for a in args)
    size += sum(int(np.prod(o.shape)) * o.dtype.itemsize for o in outs)
    single = len(outs) == 1
    return pl.pallas_call(
        kernel,
        out_shape=outs[0] if single else outs,
        in_specs=in_specs,
        out_specs=out_spec if single else [out_spec] * len(outs) if out_spec is VMEM else out_spec,
        scratch_shapes=list(scratch),
        cost_estimate=pl.CostEstimate(flops=flops, bytes_accessed=size, transcendentals=0),
        compiler_params=pltpu.CompilerParams(vmem_limit_bytes=vmem),
        name=name,
    )(*args)


def first_request():
    return lax.axis_index("req") * REQ_DEV


def fan_kernel(slot_ref, x_ref, out_ref, slot_out_ref, done):
    copy = pltpu.make_async_copy(slot_ref, slot_out_ref, done)
    copy.start()
    for at in range(4):
        out_ref[at] = x_ref[...]
    copy.wait()


def pack_kernel(slot_ref, x_ref, out_ref, first_ref):
    first = first_request()
    first_ref[0] = first
    for q in range(REQ_DEV):
        out_ref[slot_ref[first + q] // REQ_DEV] = x_ref[q]


def stage_kernel(*refs):
    count = len(refs) // 2
    done = refs[-1]
    copies = [
        pltpu.make_async_copy(refs[at], refs[count + at], done.at[at]) for at in range(count)
    ]
    for copy in copies:
        copy.start()
    for copy in copies:
        copy.wait()


def mix_kernel(
    source_ref, count_ref, got_ref, shift_ref, blend_ref, proj_ref, decay_ref, learn_ref, spread_ref,
    out_ref, new_shift_ref, tokens,
):
    for page in range(REQ_DEV):
        tile = got_ref[source_ref[page]].astype(F32)
        for part in range(4):
            tokens[part, pl.ds(page, TS, stride=REQ_DEV), :] = tile[part * TS:(part + 1) * TS]
    current = jnp.concatenate([tokens[part] for part in range(4)], axis=1)
    before = jnp.concatenate([shift_ref[...], current[:-REQ_DEV]], axis=0)
    towards = before - current

    def mixed(branch):
        return (current + towards * blend_ref[branch:branch + 1, :]).astype(BF16)

    def low_rank(rows, weight):
        return lax.dot_general(
            rows, weight, (((1,), (1,)), ((), ())), preferred_element_type=F32
        ).astype(BF16)

    value = dot(dot(mixed(3), proj_ref[2]).astype(BF16), spread_ref[...]).astype(BF16)
    recept = dot(mixed(0), proj_ref[0]).astype(BF16)
    key = dot(mixed(2), proj_ref[1]).astype(BF16)
    decay = low_rank(mixed(1), decay_ref[...])
    learn = low_rank(mixed(4), learn_ref[...])
    pad = jnp.zeros((TOK, LANES - decay.shape[1]), BF16)
    for part in range(4):
        out_ref[part, :, 0:FEATS] = recept
        out_ref[part, :, FEATS:2 * FEATS] = key
        out_ref[part, :, 2 * FEATS:DECAY_AT] = value[:, part * VALS:(part + 1) * VALS]
        out_ref[part, :, DECAY_AT:LEARN_AT] = jnp.concatenate([decay, pad], axis=1)
        out_ref[part, :, LEARN_AT:WIDTH] = jnp.concatenate([learn, pad], axis=1)
    for page in range(REQ_DEV):
        row = (count_ref[page] - 1) * REQ_DEV + page
        for part in range(4):
            new_shift_ref[page:page + 1, part * LANES:(part + 1) * LANES] = tokens[part, pl.ds(row, 1), :]


def state_kernel(
    count_ref, got_ref, state_ref, decay_ref, decay_offset_ref, learn_ref, learn_offset_ref, gain_ref,
    correction_ref, reward_ref, halves_ref, same_head_ref, head_to_lanes_ref,
    new_state_ref, reading_ref, bonus_ref, stat_ref, spread, states, factors,
):
    lane = lax.broadcasted_iota(jnp.int32, (REQ_DEV, 256), 1)
    lane_key = lane % 64 - lane // 128
    for head in range(HEADS):
        for quad in range(4):
            at = (head * 4 + quad) * REQ_DEV
            for half in range(2):
                for group in range(2):
                    start = group * 512 + (quad * 2 + half) * 8 + head
                    states[at + group * 8:at + group * 8 + 8, half * LANES:(half + 1) * LANES] = (
                        state_ref[pl.ds(start, 8, stride=64), :]
                    )
    total = got_ref[0].astype(F32)
    for part in range(1, 4):
        total = total + got_ref[part].astype(F32)
    recept = total[:, 0:FEATS]
    key = total[:, FEATS:2 * FEATS]
    value = total[:, 2 * FEATS:DECAY_AT]
    decay_low = jnp.tanh(total[:, DECAY_AT:DECAY_AT + decay_ref.shape[0]]).astype(BF16)
    learn_low = total[:, LEARN_AT:LEARN_AT + learn_ref.shape[0]].astype(BF16)
    decay_in = decay_offset_ref[...] + dot(decay_low, decay_ref[...])
    learn = jax.nn.sigmoid(learn_offset_ref[...] + dot(learn_low, learn_ref[...]))
    decay = jnp.exp(jax.nn.sigmoid(decay_in) * (-float(np.exp(-0.5))))
    halves = halves_ref[...]
    scaled = key * gain_ref[...]
    squares = scaled * scaled
    norm = dot_split(jnp.concatenate([squares[:, 0:256], squares[:, 256:512]], axis=0), halves)
    norm = jnp.concatenate([norm[0:TOK], norm[TOK:2 * TOK]], axis=1)
    key_dir = scaled * lax.rsqrt(norm + 1e-6)
    key_adj = key * (1.0 + (learn - 1.0) * correction_ref[...])
    counts = count_ref[...]
    live = jnp.concatenate([jnp.where(counts > t, 1.0, 0.0) for t in range(TS)], axis=0)
    live_wide = jnp.concatenate([live] * 4, axis=1)
    vectors = [
        key_dir,
        jnp.where(live_wide > 0, decay, 1.0),
        key_dir * learn * live_wide,
        key_adj * live_wide,
        recept * live_wide,
    ]
    low_half = lax.broadcasted_iota(jnp.int32, (TOK, LANES), 1) < 64
    for at, vector in enumerate(vectors):
        for pair in range(HEADS // 2):
            block = vector[:, pair * LANES:(pair + 1) * LANES]
            turned = pltpu.roll(block, 64, 1)
            spread[at, 2 * pair] = jnp.where(low_half, block, turned)
            spread[at, 2 * pair + 1] = jnp.where(low_half, turned, block)
    value_pair = jnp.concatenate([value, value], axis=1)
    masks = [[lane_key == head * 8 + 2 * quad for quad in range(4)] for head in range(HEADS)]

    def vector_at(at, head, t):
        row = spread[at, head, t * REQ_DEV:(t + 1) * REQ_DEV, :]
        return jnp.concatenate([jnp.concatenate([row, row], axis=1)] * 4, axis=0)

    for t in range(TS + 1):
        for head in range(HEADS):
            place = slice(head * 64, (head + 1) * 64)
            state = states[place, :]
            if t > 0:
                removed = product[head * 64:(head + 1) * 64]
                added = product[512 + head * 64:512 + (head + 1) * 64]
                state = (
                    state * vector_at(1, head, t - 1)
                    - removed * vector_at(2, head, t - 1)
                    + added * vector_at(3, head, t - 1)
                )
                if t < TS:
                    states[place, :] = state
                else:
                    for quad in range(4):
                        for half in range(2):
                            for group in range(2):
                                at = quad * REQ_DEV + group * 8
                                start = group * 512 + (quad * 2 + half) * 8 + head
                                new_state_ref[pl.ds(start, 8, stride=64), :] = state[
                                    at:at + 8, half * LANES:(half + 1) * LANES
                                ]
                query = (state * vector_at(4, head, t - 1)).astype(BF16)
                factors[1024 + head * 64:1024 + (head + 1) * 64, :] = query
            if t < TS:
                factors[place, :] = (state * vector_at(0, head, t)).astype(BF16)
                now = value_pair[t * REQ_DEV:(t + 1) * REQ_DEV]
                picked = jnp.concatenate([jnp.where(m, now, 0.0) for m in masks[head]], axis=0)
                factors[512 + head * 64:512 + (head + 1) * 64, :] = picked.astype(BF16)
        first = 0 if t < TS else 1024
        last = 1536 if t > 0 else 1024
        product = dot(factors[first:last, :], halves)
        if t > 0:
            read = product[1024 - first:]
            reading = jnp.zeros((REQ_DEV, LANES), F32)
            for head in range(HEADS):
                for quad in range(4):
                    at = (head * 4 + quad) * REQ_DEV
                    part = jnp.where(masks[head][quad], read[at:at + REQ_DEV], 0.0)
                    reading = reading + part[:, 0:LANES] + part[:, LANES:256]
            reading_ref[(t - 1) * REQ_DEV:t * REQ_DEV, :] = reading
    reward = dot_split(recept * key_adj * reward_ref[...], head_to_lanes_ref[...])
    bonus_ref[...] = reward * value * live
    reading = reading_ref[...]
    same_head = same_head_ref[...]
    head_sum = dot_split(reading, same_head)
    away = reading - head_sum * (1.0 / ROWS)
    away_sum = dot_split(away * away, same_head)
    stat = jnp.where(low_half, head_sum, away_sum)
    slot = lax.broadcasted_iota(jnp.int32, (8, LANES), 1) % 8
    packed = jnp.zeros((8, LANES), F32)
    for group in range(8):
        packed = packed + jnp.where(slot == group, stat[group * 8:(group + 1) * 8], 0.0)
    for part in range(4):
        stat_ref[part] = packed


def norm_kernel(source_ref, stat_ref, reading_ref, bonus_ref, gain_ref, unpack_ref, to_natural_ref, out_ref, rows):
    lane = lax.broadcasted_iota(jnp.int32, (8, LANES), 1)
    stats = [stat_ref[part] for part in range(4)]
    mean = (stats[0] + stats[1] + stats[2] + stats[3]) * (1.0 / CHANNEL_SPAN)
    away = pltpu.roll(stats[0] + stats[1] + stats[2] + stats[3], 64, 1)
    for part in range(4):
        gap = stats[part] * (1.0 / ROWS) - mean
        away = away + gap * gap * float(ROWS)
    scale = lax.rsqrt(jnp.where(lane < 64, away, 0.0) * (1.0 / CHANNEL_SPAN) + 0.00064)
    both = jnp.where(lane < 64, mean, pltpu.roll(scale, 64, 1))
    packed = jnp.concatenate([jnp.where(lane % 8 == group, both, 0.0) for group in range(8)], axis=0)
    high = packed.astype(BF16)
    rest = packed - high.astype(F32)
    middle = rest.astype(BF16)
    low = (rest - middle.astype(F32)).astype(BF16)
    opened = dot(jnp.concatenate([high, middle, low], axis=0), unpack_ref[...])
    opened = opened[0:TOK] + opened[TOK:2 * TOK] + opened[2 * TOK:3 * TOK]
    normed = (reading_ref[...] - opened[:, 0:LANES]) * opened[:, LANES:256] * gain_ref[...] + bonus_ref[...]
    rows[...] = dot(normed.astype(BF16), to_natural_ref[...])
    for page in range(REQ_DEV):
        out_ref[source_ref[page]] = rows[pl.ds(page, TS, stride=REQ_DEV), :].astype(BF16)


def output_kernel(slot_ref, got_ref, proj_ref, out_ref, rows):
    first = first_request()
    for q in range(REQ_DEV):
        rows[q * TS:(q + 1) * TS, :] = got_ref[slot_ref[first + q] // REQ_DEV].astype(F32)
    terms = dot(rows[...].astype(BF16), proj_ref[...]).astype(BF16)
    for head in range(4):
        for part in range(4):
            out_ref[head * 4 + part] = terms[
                head * REQ_DEV:(head + 1) * REQ_DEV, part * FEATS:(part + 1) * FEATS
            ]


def shaped(shape, dtype):
    return jax.ShapeDtypeStruct(shape, dtype)


def per_device(
    incoming_activations,
    genuine_symbol_number,
    caller_sheet_slot,
    memory_sheets,
    prior_activation_sheets,
    blend_fractions,
    first_projectors,
    fading_narrow_projector,
    fading_widen_projector,
    fading_offset,
    context_step_narrowing,
    context_step_widening,
    context_step_offset,
    erasure_address_gain,
    address_correction,
    reward_coefficients,
    groupwise_gain,
    final_projector,
):
    groups = lax.axis_size("req")
    halves, same_head, head_to_lanes, to_natural, spread_values, unpack = [
        jnp.asarray(m, BF16) for m in constant_matrices()
    ]
    tiles = incoming_activations.reshape(4, TS, 4, LANES).transpose(0, 2, 1, 3).reshape(4, 16, LANES)
    everywhere, slot_table = call(
        fan_kernel,
        [shaped((4, 4, 16, LANES), BF16), shaped(caller_sheet_slot.shape, jnp.int32)],
        [ANY, VMEM],
        (caller_sheet_slot, tiles),
        scratch=[pltpu.SemaphoreType.DMA],
        name="fan",
    )
    mine = lax.all_to_all(everywhere, "head", 0, 0, tiled=True).reshape(REQ_DEV, 16, LANES)
    packed, first = call(
        pack_kernel,
        [shaped((groups, 16, LANES), BF16), shaped((1,), jnp.int32)],
        [SMEM, VMEM],
        (slot_table, mine),
        name="pack",
        out_spec=[VMEM, SMEM],
    )
    slots, valid, gain, reward, first, *weights = lax.optimization_barrier(
        (
            caller_sheet_slot, genuine_symbol_number, groupwise_gain, reward_coefficients, first,
            prior_activation_sheets, blend_fractions, first_projectors, fading_narrow_projector.T,
            context_step_narrowing.T, spread_values,
        )
    )
    weights = call(
        stage_kernel,
        [shaped(w.shape, w.dtype) for w in weights],
        [ANY] * len(weights),
        weights,
        scratch=[pltpu.SemaphoreType.DMA((len(weights),))],
        name="stage",
        vmem=121 * 2**19,
    )
    pages = first + jnp.arange(REQ_DEV, dtype=jnp.int32)
    holder = slots[None, :] == pages[:, None]
    groups_of = lax.shift_right_logical(jnp.arange(slots.shape[0], dtype=jnp.int32), 4)
    source = jnp.sum(jnp.where(holder, groups_of[None, :], 0), axis=1)
    count = jnp.sum(jnp.where(holder, valid[None, :], 0), axis=1)
    count_wide = jnp.broadcast_to(count[:, None], (REQ_DEV, LANES))
    gain = gain.reshape(HEADS, 8, 2).transpose(2, 0, 1).reshape(1, VALS)
    reward = reward.reshape(1, FEATS)
    got = lax.all_to_all(packed, "req", 0, 0, tiled=True)
    got, source, count, count_wide, gain, reward, *weights = lax.optimization_barrier(
        (got, source, count, count_wide, gain, reward, *weights)
    )
    partial, new_shift = call(
        mix_kernel,
        [shaped((4, TOK, WIDTH), BF16), shaped((REQ_DEV, FEATS), F32)],
        [SMEM] * 2 + [VMEM] * 7,
        (source, count, got, *weights),
        scratch=[pltpu.VMEM((4, TOK, LANES), F32)],
        flops=2 * TOK * FEATS * (3 * FEATS + 192),
        name="mix",
    )
    sheets = memory_sheets.reshape(REQ_DEV, HEADS, 8, LANES).transpose(0, 2, 1, 3)
    sheets = sheets.reshape(REQ_DEV * HEADS * 8, LANES)
    sums = lax.all_to_all(partial, "row", 0, 0, tiled=True)
    new_state, reading, bonus, stat = call(
        state_kernel,
        [
            shaped((REQ_DEV * HEADS * 8, LANES), F32),
            shaped((TOK, LANES), F32),
            shaped((TOK, LANES), F32),
            shaped((4, 8, LANES), F32),
        ],
        [VMEM] * 13,
        (
            count_wide,
            sums,
            sheets,
            fading_widen_projector,
            fading_offset[None],
            context_step_widening,
            context_step_offset[None],
            erasure_address_gain[None],
            address_correction[None],
            reward,
            halves,
            same_head,
            head_to_lanes,
        ),
        scratch=[pltpu.VMEM((5, HEADS, TOK, LANES), F32), pltpu.VMEM((512, 256), F32), pltpu.VMEM((1536, 256), BF16)],
        flops=2 * 3 * TS * 512 * 256 * 256,
        name="state",
    )
    stats = lax.all_to_all(stat, "row", 0, 0, tiled=True)
    leaving = call(
        norm_kernel,
        [shaped((groups, TS, LANES), BF16)],
        [SMEM] + [VMEM] * 6,
        (source, stats, reading, bonus, gain, unpack, to_natural),
        scratch=[pltpu.VMEM((TOK, LANES), F32)],
        name="norm",
    )
    back = lax.all_to_all(leaving, "req", 0, 0, tiled=True)
    terms = call(
        output_kernel,
        [shaped((16, 16, FEATS), BF16)],
        [SMEM, VMEM, VMEM],
        (slot_table, back, final_projector.reshape(VALS, 4 * FEATS)),
        scratch=[pltpu.VMEM((TOK, LANES), F32)],
        flops=2 * TOK * VALS * 4 * FEATS,
        name="output",
    )
    arrived = lax.all_to_all(terms, ("head", "row"), 0, 0, tiled=True)
    mixed = jnp.sum(arrived.astype(F32), axis=0).astype(BF16).reshape(4, TS, FEATS)
    new_state = new_state.reshape(REQ_DEV, 8, HEADS, LANES).transpose(0, 2, 1, 3)
    return (mixed, new_state.reshape(REQ_DEV, HEADS, 8 * LANES), new_shift)


def solution(mesh):
    placed = (
        P(("req", "head"), None, "row"),
        P(),
        P(),
        P("req", "head", "row"),
        P("req", "row"),
        P(None, "row"),
        P(None, "row", "head"),
        P("row", None),
        P(None, "head"),
        P("head"),
        P("row", None),
        P(None, "head"),
        P("head"),
        P("head"),
        P("head"),
        P("head", None),
        P("head", "row"),
        P("head", "row", None),
    )
    return jax.shard_map(
        per_device,
        mesh=mesh,
        in_specs=placed,
        out_specs=(P(("req", "head"), None, "row"), P("req", "head", "row"), P("req", "row")),
        check_vma=False,
    )
```

```python
import functools

import jax
import jax.numpy as jnp
import numpy as np
from jax import lax
from jax.experimental import pallas as pl
from jax.experimental.pallas import tpu as pltpu
from jax.sharding import PartitionSpec as P

CHANNEL_SPAN = 64
TS = 4
REQ_DEV = 16
HEADS = 8
ROWS = 16
FEATS = HEADS * CHANNEL_SPAN
VALS = HEADS * ROWS
TOK = REQ_DEV * TS
LANES = 128
DECAY_AT = 2 * FEATS + VALS
LEARN_AT = DECAY_AT + LANES
WIDTH = LEARN_AT + LANES
F32 = jnp.float32
BF16 = jnp.bfloat16
VMEM = pl.BlockSpec(memory_space=pltpu.VMEM)
SMEM = pl.BlockSpec(memory_space=pltpu.SMEM)
ANY = pl.BlockSpec(memory_space=pl.ANY)


def value_lane(head, row):
    return (row % 2) * 64 + head * 8 + row // 2


def constant_matrices():
    lanes = np.arange(256)
    halves = (lanes[:, None] // 64 == lanes[None, :] // 64).astype(np.float32)
    c = np.arange(VALS)
    lane_head = (c % 64) // 8
    same_head = (lane_head[:, None] == lane_head[None, :]).astype(np.float32)
    head_to_lanes = (np.arange(FEATS)[:, None] // 64 == lane_head[None, :]).astype(np.float32)
    to_natural = np.zeros((VALS, VALS), np.float32)
    spread_values = np.zeros((FEATS, FEATS), np.float32)
    for head in range(HEADS):
        for row in range(ROWS):
            to_natural[value_lane(head, row), head * ROWS + row] = 1
            for part in range(4):
                spread_values[head * 64 + part * ROWS + row, part * VALS + value_lane(head, row)] = 1
    unpack = np.zeros((LANES, 2, LANES), np.float32)
    for side in range(2):
        unpack[side * 64:(side + 1) * 64, side] = same_head[side * 64:(side + 1) * 64]
    return halves, same_head, head_to_lanes, to_natural, spread_values, unpack.reshape(LANES, 256)


def dot(a, b):
    return jnp.dot(a, b, preferred_element_type=F32)


def dot_split(a, b):
    high = a.astype(BF16)
    low = (a - high.astype(F32)).astype(BF16)
    return dot(high, b) + dot(low, b)


def call(kernel, outs, in_specs, args, scratch=(), flops=0, name=None, out_spec=VMEM):
    size = sum(int(np.prod(a.shape)) * a.dtype.itemsize for a in args)
    size += sum(int(np.prod(o.shape)) * o.dtype.itemsize for o in outs)
    single = len(outs) == 1
    return pl.pallas_call(
        kernel,
        out_shape=outs[0] if single else outs,
        in_specs=in_specs,
        out_specs=out_spec if single else [out_spec] * len(outs),
        scratch_shapes=list(scratch),
        cost_estimate=pl.CostEstimate(flops=flops, bytes_accessed=size, transcendentals=0),
        compiler_params=pltpu.CompilerParams(vmem_limit_bytes=32 * 2**20),
        name=name,
    )(*args)


def fan_kernel(x_ref, out_ref, done):
    copies = [pltpu.make_async_copy(x_ref, out_ref.at[at], done.at[at]) for at in range(4)]
    for copy in copies:
        copy.start()
    for copy in copies:
        copy.wait()


def pack_kernel(slot_ref, first_ref, x_ref, out_ref):
    for q in range(REQ_DEV):
        out_ref[slot_ref[first_ref[0] + q] // REQ_DEV] = x_ref[q]


def mix_kernel(
    source_ref, count_ref, got_ref, shift_ref, blend_ref, proj_ref, decay_ref, learn_ref, spread_ref,
    out_ref, new_shift_ref, tokens,
):
    for page in range(REQ_DEV):
        tile = got_ref[source_ref[page]].astype(F32)
        for part in range(4):
            tokens[part, pl.ds(page, TS, stride=REQ_DEV), :] = tile[part * TS:(part + 1) * TS]
    current = jnp.concatenate([tokens[part] for part in range(4)], axis=1)
    before = jnp.concatenate([shift_ref[...], current[:-REQ_DEV]], axis=0)
    towards = before - current

    def mixed(branch):
        return (current + towards * blend_ref[branch:branch + 1, :]).astype(BF16)

    def low_rank(rows, weight):
        return lax.dot_general(
            rows, weight, (((1,), (1,)), ((), ())), preferred_element_type=F32
        ).astype(BF16)

    value = dot(dot(mixed(3), proj_ref[2]).astype(BF16), spread_ref[...]).astype(BF16)
    recept = dot(mixed(0), proj_ref[0]).astype(BF16)
    key = dot(mixed(2), proj_ref[1]).astype(BF16)
    decay = low_rank(mixed(1), decay_ref[...])
    learn = low_rank(mixed(4), learn_ref[...])
    pad = jnp.zeros((TOK, LANES - decay.shape[1]), BF16)
    for part in range(4):
        out_ref[part, :, 0:FEATS] = recept
        out_ref[part, :, FEATS:2 * FEATS] = key
        out_ref[part, :, 2 * FEATS:DECAY_AT] = value[:, part * VALS:(part + 1) * VALS]
        out_ref[part, :, DECAY_AT:LEARN_AT] = jnp.concatenate([decay, pad], axis=1)
        out_ref[part, :, LEARN_AT:WIDTH] = jnp.concatenate([learn, pad], axis=1)
    for page in range(REQ_DEV):
        row = (count_ref[page] - 1) * REQ_DEV + page
        for part in range(4):
            new_shift_ref[page:page + 1, part * LANES:(part + 1) * LANES] = tokens[part, pl.ds(row, 1), :]


def state_kernel(
    count_ref, got_ref, state_ref, decay_ref, decay_offset_ref, learn_ref, learn_offset_ref, gain_ref,
    correction_ref, reward_ref, halves_ref, same_head_ref, head_to_lanes_ref,
    new_state_ref, reading_ref, bonus_ref, stat_ref, spread, states, factors,
):
    lane = lax.broadcasted_iota(jnp.int32, (REQ_DEV, 256), 1)
    lane_key = lane % 64 - lane // 128
    for head in range(HEADS):
        for quad in range(4):
            at = (head * 4 + quad) * REQ_DEV
            for half in range(2):
                for group in range(2):
                    start = group * 512 + (quad * 2 + half) * 8 + head
                    states[at + group * 8:at + group * 8 + 8, half * LANES:(half + 1) * LANES] = (
                        state_ref[pl.ds(start, 8, stride=64), :]
                    )
    total = got_ref[0].astype(F32)
    for part in range(1, 4):
        total = total + got_ref[part].astype(F32)
    recept = total[:, 0:FEATS]
    key = total[:, FEATS:2 * FEATS]
    value = total[:, 2 * FEATS:DECAY_AT]
    decay_low = jnp.tanh(total[:, DECAY_AT:DECAY_AT + decay_ref.shape[0]]).astype(BF16)
    learn_low = total[:, LEARN_AT:LEARN_AT + learn_ref.shape[0]].astype(BF16)
    decay_in = decay_offset_ref[...] + dot(decay_low, decay_ref[...])
    learn = jax.nn.sigmoid(learn_offset_ref[...] + dot(learn_low, learn_ref[...]))
    decay = jnp.exp(jax.nn.sigmoid(decay_in) * (-float(np.exp(-0.5))))
    halves = halves_ref[...]
    scaled = key * gain_ref[...]
    squares = scaled * scaled
    norm = dot_split(jnp.concatenate([squares[:, 0:256], squares[:, 256:512]], axis=0), halves)
    norm = jnp.concatenate([norm[0:TOK], norm[TOK:2 * TOK]], axis=1)
    key_dir = scaled * lax.rsqrt(norm + 1e-6)
    key_adj = key * (1.0 + (learn - 1.0) * correction_ref[...])
    counts = count_ref[...]
    live = jnp.concatenate([jnp.where(counts > t, 1.0, 0.0) for t in range(TS)], axis=0)
    live_wide = jnp.concatenate([live] * 4, axis=1)
    vectors = [
        key_dir,
        jnp.where(live_wide > 0, decay, 1.0),
        key_dir * learn * live_wide,
        key_adj * live_wide,
        recept * live_wide,
    ]
    low_half = lax.broadcasted_iota(jnp.int32, (TOK, LANES), 1) < 64
    for at, vector in enumerate(vectors):
        for pair in range(HEADS // 2):
            block = vector[:, pair * LANES:(pair + 1) * LANES]
            turned = pltpu.roll(block, 64, 1)
            spread[at, 2 * pair] = jnp.where(low_half, block, turned)
            spread[at, 2 * pair + 1] = jnp.where(low_half, turned, block)
    value_pair = jnp.concatenate([value, value], axis=1)
    masks = [[lane_key == head * 8 + 2 * quad for quad in range(4)] for head in range(HEADS)]

    def vector_at(at, head, t):
        row = spread[at, head, t * REQ_DEV:(t + 1) * REQ_DEV, :]
        return jnp.concatenate([jnp.concatenate([row, row], axis=1)] * 4, axis=0)

    for t in range(TS + 1):
        for head in range(HEADS):
            place = slice(head * 64, (head + 1) * 64)
            state = states[place, :]
            if t > 0:
                removed = product[head * 64:(head + 1) * 64]
                added = product[512 + head * 64:512 + (head + 1) * 64]
                state = (
                    state * vector_at(1, head, t - 1)
                    - removed * vector_at(2, head, t - 1)
                    + added * vector_at(3, head, t - 1)
                )
                if t < TS:
                    states[place, :] = state
                else:
                    for quad in range(4):
                        for half in range(2):
                            for group in range(2):
                                at = quad * REQ_DEV + group * 8
                                start = group * 512 + (quad * 2 + half) * 8 + head
                                new_state_ref[pl.ds(start, 8, stride=64), :] = state[
                                    at:at + 8, half * LANES:(half + 1) * LANES
                                ]
                query = (state * vector_at(4, head, t - 1)).astype(BF16)
                factors[1024 + head * 64:1024 + (head + 1) * 64, :] = query
            if t < TS:
                factors[place, :] = (state * vector_at(0, head, t)).astype(BF16)
                now = value_pair[t * REQ_DEV:(t + 1) * REQ_DEV]
                picked = jnp.concatenate([jnp.where(m, now, 0.0) for m in masks[head]], axis=0)
                factors[512 + head * 64:512 + (head + 1) * 64, :] = picked.astype(BF16)
        first = 0 if t < TS else 1024
        last = 1536 if t > 0 else 1024
        product = dot(factors[first:last, :], halves)
        if t > 0:
            read = product[1024 - first:]
            reading = jnp.zeros((REQ_DEV, LANES), F32)
            for head in range(HEADS):
                for quad in range(4):
                    at = (head * 4 + quad) * REQ_DEV
                    part = jnp.where(masks[head][quad], read[at:at + REQ_DEV], 0.0)
                    reading = reading + part[:, 0:LANES] + part[:, LANES:256]
            reading_ref[(t - 1) * REQ_DEV:t * REQ_DEV, :] = reading
    reward = dot_split(recept * key_adj * reward_ref[...], head_to_lanes_ref[...])
    bonus_ref[...] = reward * value * live
    reading = reading_ref[...]
    same_head = same_head_ref[...]
    head_sum = dot_split(reading, same_head)
    away = reading - head_sum * (1.0 / ROWS)
    away_sum = dot_split(away * away, same_head)
    stat = jnp.where(low_half, head_sum, away_sum)
    slot = lax.broadcasted_iota(jnp.int32, (8, LANES), 1) % 8
    packed = jnp.zeros((8, LANES), F32)
    for group in range(8):
        packed = packed + jnp.where(slot == group, stat[group * 8:(group + 1) * 8], 0.0)
    for part in range(4):
        stat_ref[part] = packed


def norm_kernel(source_ref, stat_ref, reading_ref, bonus_ref, gain_ref, unpack_ref, to_natural_ref, out_ref, rows):
    lane = lax.broadcasted_iota(jnp.int32, (8, LANES), 1)
    stats = [stat_ref[part] for part in range(4)]
    mean = (stats[0] + stats[1] + stats[2] + stats[3]) * (1.0 / CHANNEL_SPAN)
    away = pltpu.roll(stats[0] + stats[1] + stats[2] + stats[3], 64, 1)
    for part in range(4):
        gap = stats[part] * (1.0 / ROWS) - mean
        away = away + gap * gap * float(ROWS)
    scale = lax.rsqrt(jnp.where(lane < 64, away, 0.0) * (1.0 / CHANNEL_SPAN) + 0.00064)
    both = jnp.where(lane < 64, mean, pltpu.roll(scale, 64, 1))
    packed = jnp.concatenate([jnp.where(lane % 8 == group, both, 0.0) for group in range(8)], axis=0)
    high = packed.astype(BF16)
    rest = packed - high.astype(F32)
    middle = rest.astype(BF16)
    low = (rest - middle.astype(F32)).astype(BF16)
    opened = dot(jnp.concatenate([high, middle, low], axis=0), unpack_ref[...])
    opened = opened[0:TOK] + opened[TOK:2 * TOK] + opened[2 * TOK:3 * TOK]
    normed = (reading_ref[...] - opened[:, 0:LANES]) * opened[:, LANES:256] * gain_ref[...] + bonus_ref[...]
    rows[...] = dot(normed.astype(BF16), to_natural_ref[...])
    for page in range(REQ_DEV):
        out_ref[source_ref[page]] = rows[pl.ds(page, TS, stride=REQ_DEV), :].astype(BF16)


def output_kernel(slot_ref, first_ref, got_ref, proj_ref, out_ref, rows):
    for q in range(REQ_DEV):
        rows[q * TS:(q + 1) * TS, :] = got_ref[slot_ref[first_ref[0] + q] // REQ_DEV].astype(F32)
    terms = dot(rows[...].astype(BF16), proj_ref[...]).astype(BF16)
    for head in range(4):
        for part in range(4):
            out_ref[head * 4 + part] = terms[
                head * REQ_DEV:(head + 1) * REQ_DEV, part * FEATS:(part + 1) * FEATS
            ]


def shaped(shape, dtype):
    return jax.ShapeDtypeStruct(shape, dtype)


def per_device(
    incoming_activations,
    genuine_symbol_number,
    caller_sheet_slot,
    memory_sheets,
    prior_activation_sheets,
    blend_fractions,
    first_projectors,
    fading_narrow_projector,
    fading_widen_projector,
    fading_offset,
    context_step_narrowing,
    context_step_widening,
    context_step_offset,
    erasure_address_gain,
    address_correction,
    reward_coefficients,
    groupwise_gain,
    final_projector,
):
    groups = lax.axis_size("req")
    halves, same_head, head_to_lanes, to_natural, spread_values, unpack = [
        jnp.asarray(m, BF16) for m in constant_matrices()
    ]
    first = lax.axis_index("req") * REQ_DEV
    pages = first + jnp.arange(REQ_DEV, dtype=jnp.int32)
    holder = caller_sheet_slot[None, :] == pages[:, None]
    groups_of = lax.shift_right_logical(jnp.arange(caller_sheet_slot.shape[0], dtype=jnp.int32), 4)
    source = jnp.sum(jnp.where(holder, groups_of[None, :], 0), axis=1)
    count = jnp.sum(jnp.where(holder, genuine_symbol_number[None, :], 0), axis=1)
    count_wide = jnp.broadcast_to(count[:, None], (REQ_DEV, LANES))
    first = first.astype(jnp.int32)[None]
    gain = groupwise_gain.reshape(HEADS, 8, 2).transpose(2, 0, 1).reshape(1, VALS)
    reward = reward_coefficients.reshape(1, FEATS)

    tiles = incoming_activations.reshape(4, TS, 4, LANES).transpose(0, 2, 1, 3).reshape(4, 16, LANES)
    everywhere = call(
        fan_kernel,
        [shaped((4, 4, 16, LANES), BF16)],
        [pl.BlockSpec(memory_space=pltpu.HBM)],
        (tiles,),
        scratch=[pltpu.SemaphoreType.DMA((4,))],
        flops=6 * 10**9,
        name="fan",
        out_spec=ANY,
    )
    mine = lax.all_to_all(everywhere, "head", 0, 0, tiled=True).reshape(REQ_DEV, 16, LANES)
    mine, source, count, count_wide, gain, reward = lax.optimization_barrier(
        (mine, source, count, count_wide, gain, reward)
    )
    packed = call(
        pack_kernel,
        [shaped((groups, 16, LANES), BF16)],
        [SMEM, SMEM, VMEM],
        (caller_sheet_slot, first, mine),
        flops=6 * 10**9,
        name="pack",
    )
    got = lax.all_to_all(packed, "req", 0, 0, tiled=True)
    partial, new_shift = call(
        mix_kernel,
        [shaped((4, TOK, WIDTH), BF16), shaped((REQ_DEV, FEATS), F32)],
        [SMEM] * 2 + [VMEM] * 7,
        (
            source, count, got, prior_activation_sheets, blend_fractions, first_projectors,
            fading_narrow_projector.T, context_step_narrowing.T, spread_values,
        ),
        scratch=[pltpu.VMEM((4, TOK, LANES), F32)],
        flops=2 * TOK * FEATS * (3 * FEATS + 192),
        name="mix",
    )
    sheets = memory_sheets.reshape(REQ_DEV, HEADS, 8, LANES).transpose(0, 2, 1, 3)
    sheets = sheets.reshape(REQ_DEV * HEADS * 8, LANES)
    sums = lax.all_to_all(partial, "row", 0, 0, tiled=True)
    new_state, reading, bonus, stat = call(
        state_kernel,
        [
            shaped((REQ_DEV * HEADS * 8, LANES), F32),
            shaped((TOK, LANES), F32),
            shaped((TOK, LANES), F32),
            shaped((4, 8, LANES), F32),
        ],
        [VMEM] * 13,
        (
            count_wide,
            sums,
            sheets,
            fading_widen_projector,
            fading_offset[None],
            context_step_widening,
            context_step_offset[None],
            erasure_address_gain[None],
            address_correction[None],
            reward,
            halves,
            same_head,
            head_to_lanes,
        ),
        scratch=[pltpu.VMEM((5, HEADS, TOK, LANES), F32), pltpu.VMEM((512, 256), F32), pltpu.VMEM((1536, 256), BF16)],
        flops=2 * 3 * TS * 512 * 256 * 256,
        name="state",
    )
    stats = lax.all_to_all(stat, "row", 0, 0, tiled=True)
    leaving = call(
        norm_kernel,
        [shaped((groups, TS, LANES), BF16)],
        [SMEM] + [VMEM] * 6,
        (source, stats, reading, bonus, gain, unpack, to_natural),
        scratch=[pltpu.VMEM((TOK, LANES), F32)],
        name="norm",
    )
    back = lax.all_to_all(leaving, "req", 0, 0, tiled=True)
    terms = call(
        output_kernel,
        [shaped((16, 16, FEATS), BF16)],
        [SMEM, SMEM, VMEM, VMEM],
        (caller_sheet_slot, first, back, final_projector.reshape(VALS, 4 * FEATS)),
        scratch=[pltpu.VMEM((TOK, LANES), F32)],
        flops=2 * TOK * VALS * 4 * FEATS,
        name="output",
    )
    arrived = lax.all_to_all(terms, ("head", "row"), 0, 0, tiled=True)
    mixed = jnp.sum(arrived.astype(F32), axis=0).astype(BF16).reshape(4, TS, FEATS)
    new_state = new_state.reshape(REQ_DEV, 8, HEADS, LANES).transpose(0, 2, 1, 3)
    return (mixed, new_state.reshape(REQ_DEV, HEADS, 8 * LANES), new_shift)


def solution(mesh):
    placed = (
        P(("req", "head"), None, "row"),
        P(),
        P(),
        P("req", "head", "row"),
        P("req", "row"),
        P(None, "row"),
        P(None, "row", "head"),
        P("row", None),
        P(None, "head"),
        P("head"),
        P("row", None),
        P(None, "head"),
        P("head"),
        P("head"),
        P("head"),
        P("head", None),
        P("head", "row"),
        P("head", "row", None),
    )
    return jax.shard_map(
        per_device,
        mesh=mesh,
        in_specs=placed,
        out_specs=(P(("req", "head"), None, "row"), P("req", "head", "row"), P("req", "row")),
        check_vma=False,
    )
```

```python
import functools

import jax
import jax.numpy as jnp
import numpy as np
from jax import lax
from jax.experimental import pallas as pl
from jax.experimental.pallas import tpu as pltpu
from jax.sharding import PartitionSpec as P

CHANNEL_SPAN = 64
TS = 4
REQ_DEV = 16
HEADS = 8
ROWS = 16
FEATS = HEADS * CHANNEL_SPAN
VALS = HEADS * ROWS
TOK = REQ_DEV * TS
LANES = 128
DECAY_AT = 2 * FEATS + VALS
LEARN_AT = DECAY_AT + LANES
WIDTH = LEARN_AT + LANES
F32 = jnp.float32
BF16 = jnp.bfloat16
FIRST_A, FIRST_B, FIRST_C, FIRST_D, FIRST_E, FIRST_F = 2, 17, 2, 2, 17, 10
VMEM = pl.BlockSpec(memory_space=pltpu.VMEM)
SMEM = pl.BlockSpec(memory_space=pltpu.SMEM)
ANY = pl.BlockSpec(memory_space=pl.ANY)


def value_lane(head, row):
    return (row % 2) * 64 + head * 8 + row // 2


def constant_matrices():
    lanes = np.arange(256)
    halves = (lanes[:, None] // 64 == lanes[None, :] // 64).astype(np.float32)
    c = np.arange(VALS)
    lane_head = (c % 64) // 8
    same_head = (lane_head[:, None] == lane_head[None, :]).astype(np.float32)
    head_to_lanes = (np.arange(FEATS)[:, None] // 64 == lane_head[None, :]).astype(np.float32)
    to_natural = np.zeros((VALS, VALS), np.float32)
    spread_values = np.zeros((FEATS, FEATS), np.float32)
    for head in range(HEADS):
        for row in range(ROWS):
            to_natural[value_lane(head, row), head * ROWS + row] = 1
            for part in range(4):
                spread_values[head * 64 + part * ROWS + row, part * VALS + value_lane(head, row)] = 1
    unpack = np.zeros((LANES, 2, LANES), np.float32)
    for side in range(2):
        unpack[side * 64:(side + 1) * 64, side] = same_head[side * 64:(side + 1) * 64]
    return halves, same_head, head_to_lanes, to_natural, spread_values, unpack.reshape(LANES, 256)


def dot(a, b):
    return jnp.dot(a, b, preferred_element_type=F32)


def dot_split(a, b):
    high = a.astype(BF16)
    low = (a - high.astype(F32)).astype(BF16)
    return dot(high, b) + dot(low, b)


def exchange(x, axes, first):
    order = [[k ^ first for k in range(x.shape[0])]] if first else None
    return lax.all_to_all(x, axes, 0, 0, tiled=True, axis_index_groups=order)


def call(kernel, outs, in_specs, args, scratch=(), flops=0, name=None, out_spec=VMEM):
    size = sum(int(np.prod(a.shape)) * a.dtype.itemsize for a in args)
    size += sum(int(np.prod(o.shape)) * o.dtype.itemsize for o in outs)
    single = len(outs) == 1
    return pl.pallas_call(
        kernel,
        out_shape=outs[0] if single else outs,
        in_specs=in_specs,
        out_specs=out_spec if single else [out_spec] * len(outs),
        scratch_shapes=list(scratch),
        cost_estimate=pl.CostEstimate(flops=flops, bytes_accessed=size, transcendentals=0),
        compiler_params=pltpu.CompilerParams(vmem_limit_bytes=32 * 2**20),
        name=name,
    )(*args)


def fan_kernel(x_ref, out_ref, done):
    copies = [pltpu.make_async_copy(x_ref, out_ref.at[at], done.at[at]) for at in range(4)]
    for copy in copies:
        copy.start()
    for copy in copies:
        copy.wait()


def pack_kernel(slot_ref, first_ref, x_ref, out_ref):
    for q in range(REQ_DEV):
        out_ref[(slot_ref[first_ref[0] + q] // REQ_DEV) ^ FIRST_B] = x_ref[q ^ (FIRST_A * 4)]


def mix_kernel(
    source_ref, count_ref, got_ref, shift_ref, blend_ref, proj_ref, decay_ref, learn_ref, spread_ref,
    out_ref, new_shift_ref, tokens,
):
    for page in range(REQ_DEV):
        tile = got_ref[source_ref[page] ^ FIRST_B].astype(F32)
        for part in range(4):
            tokens[part, pl.ds(page, TS, stride=REQ_DEV), :] = tile[part * TS:(part + 1) * TS]
    current = jnp.concatenate([tokens[part] for part in range(4)], axis=1)
    before = jnp.concatenate([shift_ref[...], current[:-REQ_DEV]], axis=0)
    towards = before - current

    def mixed(branch):
        return (current + towards * blend_ref[branch:branch + 1, :]).astype(BF16)

    def low_rank(rows, weight):
        return lax.dot_general(
            rows, weight, (((1,), (1,)), ((), ())), preferred_element_type=F32
        ).astype(BF16)

    value = dot(dot(mixed(3), proj_ref[2]).astype(BF16), spread_ref[...]).astype(BF16)
    recept = dot(mixed(0), proj_ref[0]).astype(BF16)
    key = dot(mixed(2), proj_ref[1]).astype(BF16)
    decay = low_rank(mixed(1), decay_ref[...])
    learn = low_rank(mixed(4), learn_ref[...])
    pad = jnp.zeros((TOK, LANES - decay.shape[1]), BF16)
    for part in range(4):
        out_ref[part, :, 0:FEATS] = recept
        out_ref[part, :, FEATS:2 * FEATS] = key
        row = part ^ FIRST_C
        out_ref[part, :, 2 * FEATS:DECAY_AT] = value[:, row * VALS:(row + 1) * VALS]
        out_ref[part, :, DECAY_AT:LEARN_AT] = jnp.concatenate([decay, pad], axis=1)
        out_ref[part, :, LEARN_AT:WIDTH] = jnp.concatenate([learn, pad], axis=1)
    for page in range(REQ_DEV):
        row = (count_ref[page] - 1) * REQ_DEV + page
        for part in range(4):
            new_shift_ref[page:page + 1, part * LANES:(part + 1) * LANES] = tokens[part, pl.ds(row, 1), :]


def state_kernel(
    count_ref, got_ref, state_ref, decay_ref, decay_offset_ref, learn_ref, learn_offset_ref, gain_ref,
    correction_ref, reward_ref, halves_ref, same_head_ref, head_to_lanes_ref,
    new_state_ref, reading_ref, bonus_ref, stat_ref, spread, states, factors,
):
    lane = lax.broadcasted_iota(jnp.int32, (REQ_DEV, 256), 1)
    lane_key = lane % 64 - lane // 128
    for head in range(HEADS):
        for quad in range(4):
            at = (head * 4 + quad) * REQ_DEV
            for half in range(2):
                for group in range(2):
                    start = group * 512 + (quad * 2 + half) * 8 + head
                    states[at + group * 8:at + group * 8 + 8, half * LANES:(half + 1) * LANES] = (
                        state_ref[pl.ds(start, 8, stride=64), :]
                    )
    total = got_ref[0].astype(F32)
    for part in range(1, 4):
        total = total + got_ref[part].astype(F32)
    recept = total[:, 0:FEATS]
    key = total[:, FEATS:2 * FEATS]
    value = total[:, 2 * FEATS:DECAY_AT]
    decay_low = jnp.tanh(total[:, DECAY_AT:DECAY_AT + decay_ref.shape[0]]).astype(BF16)
    learn_low = total[:, LEARN_AT:LEARN_AT + learn_ref.shape[0]].astype(BF16)
    decay_in = decay_offset_ref[...] + dot(decay_low, decay_ref[...])
    learn = jax.nn.sigmoid(learn_offset_ref[...] + dot(learn_low, learn_ref[...]))
    decay = jnp.exp(jax.nn.sigmoid(decay_in) * (-float(np.exp(-0.5))))
    halves = halves_ref[...]
    scaled = key * gain_ref[...]
    squares = scaled * scaled
    norm = dot_split(jnp.concatenate([squares[:, 0:256], squares[:, 256:512]], axis=0), halves)
    norm = jnp.concatenate([norm[0:TOK], norm[TOK:2 * TOK]], axis=1)
    key_dir = scaled * lax.rsqrt(norm + 1e-6)
    key_adj = key * (1.0 + (learn - 1.0) * correction_ref[...])
    counts = count_ref[...]
    live = jnp.concatenate([jnp.where(counts > t, 1.0, 0.0) for t in range(TS)], axis=0)
    live_wide = jnp.concatenate([live] * 4, axis=1)
    vectors = [
        key_dir,
        jnp.where(live_wide > 0, decay, 1.0),
        key_dir * learn * live_wide,
        key_adj * live_wide,
        recept * live_wide,
    ]
    low_half = lax.broadcasted_iota(jnp.int32, (TOK, LANES), 1) < 64
    for at, vector in enumerate(vectors):
        for pair in range(HEADS // 2):
            block = vector[:, pair * LANES:(pair + 1) * LANES]
            turned = pltpu.roll(block, 64, 1)
            spread[at, 2 * pair] = jnp.where(low_half, block, turned)
            spread[at, 2 * pair + 1] = jnp.where(low_half, turned, block)
    value_pair = jnp.concatenate([value, value], axis=1)
    masks = [[lane_key == head * 8 + 2 * quad for quad in range(4)] for head in range(HEADS)]

    def vector_at(at, head, t):
        row = spread[at, head, t * REQ_DEV:(t + 1) * REQ_DEV, :]
        return jnp.concatenate([jnp.concatenate([row, row], axis=1)] * 4, axis=0)

    for t in range(TS + 1):
        for head in range(HEADS):
            place = slice(head * 64, (head + 1) * 64)
            state = states[place, :]
            if t > 0:
                removed = product[head * 64:(head + 1) * 64]
                added = product[512 + head * 64:512 + (head + 1) * 64]
                state = (
                    state * vector_at(1, head, t - 1)
                    - removed * vector_at(2, head, t - 1)
                    + added * vector_at(3, head, t - 1)
                )
                if t < TS:
                    states[place, :] = state
                else:
                    for quad in range(4):
                        for half in range(2):
                            for group in range(2):
                                at = quad * REQ_DEV + group * 8
                                start = group * 512 + (quad * 2 + half) * 8 + head
                                new_state_ref[pl.ds(start, 8, stride=64), :] = state[
                                    at:at + 8, half * LANES:(half + 1) * LANES
                                ]
                query = (state * vector_at(4, head, t - 1)).astype(BF16)
                factors[1024 + head * 64:1024 + (head + 1) * 64, :] = query
            if t < TS:
                factors[place, :] = (state * vector_at(0, head, t)).astype(BF16)
                now = value_pair[t * REQ_DEV:(t + 1) * REQ_DEV]
                picked = jnp.concatenate([jnp.where(m, now, 0.0) for m in masks[head]], axis=0)
                factors[512 + head * 64:512 + (head + 1) * 64, :] = picked.astype(BF16)
        first = 0 if t < TS else 1024
        last = 1536 if t > 0 else 1024
        product = dot(factors[first:last, :], halves)
        if t > 0:
            read = product[1024 - first:]
            reading = jnp.zeros((REQ_DEV, LANES), F32)
            for head in range(HEADS):
                for quad in range(4):
                    at = (head * 4 + quad) * REQ_DEV
                    part = jnp.where(masks[head][quad], read[at:at + REQ_DEV], 0.0)
                    reading = reading + part[:, 0:LANES] + part[:, LANES:256]
            reading_ref[(t - 1) * REQ_DEV:t * REQ_DEV, :] = reading
    reward = dot_split(recept * key_adj * reward_ref[...], head_to_lanes_ref[...])
    bonus_ref[...] = reward * value * live
    reading = reading_ref[...]
    same_head = same_head_ref[...]
    head_sum = dot_split(reading, same_head)
    away = reading - head_sum * (1.0 / ROWS)
    away_sum = dot_split(away * away, same_head)
    stat = jnp.where(low_half, head_sum, away_sum)
    slot = lax.broadcasted_iota(jnp.int32, (8, LANES), 1) % 8
    packed = jnp.zeros((8, LANES), F32)
    for group in range(8):
        packed = packed + jnp.where(slot == group, stat[group * 8:(group + 1) * 8], 0.0)
    for part in range(4):
        stat_ref[part] = packed


def norm_kernel(source_ref, stat_ref, reading_ref, bonus_ref, gain_ref, unpack_ref, to_natural_ref, out_ref, rows):
    lane = lax.broadcasted_iota(jnp.int32, (8, LANES), 1)
    stats = [stat_ref[part] for part in range(4)]
    mean = (stats[0] + stats[1] + stats[2] + stats[3]) * (1.0 / CHANNEL_SPAN)
    away = pltpu.roll(stats[0] + stats[1] + stats[2] + stats[3], 64, 1)
    for part in range(4):
        gap = stats[part] * (1.0 / ROWS) - mean
        away = away + gap * gap * float(ROWS)
    scale = lax.rsqrt(jnp.where(lane < 64, away, 0.0) * (1.0 / CHANNEL_SPAN) + 0.00064)
    both = jnp.where(lane < 64, mean, pltpu.roll(scale, 64, 1))
    packed = jnp.concatenate([jnp.where(lane % 8 == group, both, 0.0) for group in range(8)], axis=0)
    high = packed.astype(BF16)
    rest = packed - high.astype(F32)
    middle = rest.astype(BF16)
    low = (rest - middle.astype(F32)).astype(BF16)
    opened = dot(jnp.concatenate([high, middle, low], axis=0), unpack_ref[...])
    opened = opened[0:TOK] + opened[TOK:2 * TOK] + opened[2 * TOK:3 * TOK]
    normed = (reading_ref[...] - opened[:, 0:LANES]) * opened[:, LANES:256] * gain_ref[...] + bonus_ref[...]
    rows[...] = dot(normed.astype(BF16), to_natural_ref[...])
    for page in range(REQ_DEV):
        out_ref[source_ref[page] ^ FIRST_E] = rows[pl.ds(page, TS, stride=REQ_DEV), :].astype(BF16)


def output_kernel(slot_ref, first_ref, got_ref, proj_ref, out_ref, rows):
    for q in range(REQ_DEV):
        rows[q * TS:(q + 1) * TS, :] = got_ref[
            (slot_ref[first_ref[0] + q] // REQ_DEV) ^ FIRST_E
        ].astype(F32)
    terms = dot(rows[...].astype(BF16), proj_ref[...]).astype(BF16)
    for head in range(4):
        for part in range(4):
            out_ref[(head * 4 + part) ^ FIRST_F] = terms[
                head * REQ_DEV:(head + 1) * REQ_DEV, part * FEATS:(part + 1) * FEATS
            ]


def shaped(shape, dtype):
    return jax.ShapeDtypeStruct(shape, dtype)


def per_device(
    incoming_activations,
    genuine_symbol_number,
    caller_sheet_slot,
    memory_sheets,
    prior_activation_sheets,
    blend_fractions,
    first_projectors,
    fading_narrow_projector,
    fading_widen_projector,
    fading_offset,
    context_step_narrowing,
    context_step_widening,
    context_step_offset,
    erasure_address_gain,
    address_correction,
    reward_coefficients,
    groupwise_gain,
    final_projector,
):
    groups = lax.axis_size("req")
    halves, same_head, head_to_lanes, to_natural, spread_values, unpack = [
        jnp.asarray(m, BF16) for m in constant_matrices()
    ]
    first = lax.axis_index("req") * REQ_DEV
    pages = first + jnp.arange(REQ_DEV, dtype=jnp.int32)
    holder = caller_sheet_slot[None, :] == pages[:, None]
    groups_of = lax.shift_right_logical(jnp.arange(caller_sheet_slot.shape[0], dtype=jnp.int32), 4)
    source = jnp.sum(jnp.where(holder, groups_of[None, :], 0), axis=1)
    count = jnp.sum(jnp.where(holder, genuine_symbol_number[None, :], 0), axis=1)
    count_wide = jnp.broadcast_to(count[:, None], (REQ_DEV, LANES))
    first = first.astype(jnp.int32)[None]
    gain = groupwise_gain.reshape(HEADS, 8, 2).transpose(2, 0, 1).reshape(1, VALS)
    reward = reward_coefficients.reshape(1, FEATS)

    tiles = incoming_activations.reshape(4, TS, 4, LANES).transpose(0, 2, 1, 3).reshape(4, 16, LANES)
    everywhere = call(
        fan_kernel,
        [shaped((4, 4, 16, LANES), BF16)],
        [pl.BlockSpec(memory_space=pltpu.HBM)],
        (tiles,),
        scratch=[pltpu.SemaphoreType.DMA((4,))],
        flops=6 * 10**9,
        name="fan",
        out_spec=ANY,
    )
    mine = exchange(everywhere, "head", FIRST_A).reshape(REQ_DEV, 16, LANES)
    mine, source, count, count_wide, gain, reward = lax.optimization_barrier(
        (mine, source, count, count_wide, gain, reward)
    )
    packed = call(
        pack_kernel,
        [shaped((groups, 16, LANES), BF16)],
        [SMEM, SMEM, VMEM],
        (caller_sheet_slot, first, mine),
        flops=6 * 10**9,
        name="pack",
    )
    got = exchange(packed, "req", FIRST_B)
    partial, new_shift = call(
        mix_kernel,
        [shaped((4, TOK, WIDTH), BF16), shaped((REQ_DEV, FEATS), F32)],
        [SMEM] * 2 + [VMEM] * 7,
        (
            source, count, got, prior_activation_sheets, blend_fractions, first_projectors,
            fading_narrow_projector.T, context_step_narrowing.T, spread_values,
        ),
        scratch=[pltpu.VMEM((4, TOK, LANES), F32)],
        flops=2 * TOK * FEATS * (3 * FEATS + 192),
        name="mix",
    )
    sheets = memory_sheets.reshape(REQ_DEV, HEADS, 8, LANES).transpose(0, 2, 1, 3)
    sheets = sheets.reshape(REQ_DEV * HEADS * 8, LANES)
    sums = exchange(partial, "row", FIRST_C)
    new_state, reading, bonus, stat = call(
        state_kernel,
        [
            shaped((REQ_DEV * HEADS * 8, LANES), F32),
            shaped((TOK, LANES), F32),
            shaped((TOK, LANES), F32),
            shaped((4, 8, LANES), F32),
        ],
        [VMEM] * 13,
        (
            count_wide,
            sums,
            sheets,
            fading_widen_projector,
            fading_offset[None],
            context_step_widening,
            context_step_offset[None],
            erasure_address_gain[None],
            address_correction[None],
            reward,
            halves,
            same_head,
            head_to_lanes,
        ),
        scratch=[pltpu.VMEM((5, HEADS, TOK, LANES), F32), pltpu.VMEM((512, 256), F32), pltpu.VMEM((1536, 256), BF16)],
        flops=2 * 3 * TS * 512 * 256 * 256,
        name="state",
    )
    stats = exchange(stat, "row", FIRST_D)
    leaving = call(
        norm_kernel,
        [shaped((groups, TS, LANES), BF16)],
        [SMEM] + [VMEM] * 6,
        (source, stats, reading, bonus, gain, unpack, to_natural),
        scratch=[pltpu.VMEM((TOK, LANES), F32)],
        name="norm",
    )
    back = exchange(leaving, "req", FIRST_E)
    terms = call(
        output_kernel,
        [shaped((16, 16, FEATS), BF16)],
        [SMEM, SMEM, VMEM, VMEM],
        (caller_sheet_slot, first, back, final_projector.reshape(VALS, 4 * FEATS)),
        scratch=[pltpu.VMEM((TOK, LANES), F32)],
        flops=2 * TOK * VALS * 4 * FEATS,
        name="output",
    )
    arrived = exchange(terms, ("head", "row"), FIRST_F)
    mixed = jnp.sum(arrived.astype(F32), axis=0).astype(BF16).reshape(4, TS, FEATS)
    new_state = new_state.reshape(REQ_DEV, 8, HEADS, LANES).transpose(0, 2, 1, 3)
    return (mixed, new_state.reshape(REQ_DEV, HEADS, 8 * LANES), new_shift)


def solution(mesh):
    placed = (
        P(("req", "head"), None, "row"),
        P(),
        P(),
        P("req", "head", "row"),
        P("req", "row"),
        P(None, "row"),
        P(None, "row", "head"),
        P("row", None),
        P(None, "head"),
        P("head"),
        P("row", None),
        P(None, "head"),
        P("head"),
        P("head"),
        P("head"),
        P("head", None),
        P("head", "row"),
        P("head", "row", None),
    )
    return jax.shard_map(
        per_device,
        mesh=mesh,
        in_specs=placed,
        out_specs=(P(("req", "head"), None, "row"), P("req", "head", "row"), P("req", "row")),
        check_vma=False,
    )
```

```python
import functools

import jax
import jax.numpy as jnp
import numpy as np
from jax import lax
from jax.experimental import pallas as pl
from jax.experimental.pallas import tpu as pltpu
from jax.sharding import PartitionSpec as P

CHANNEL_SPAN = 64
TS = 4
REQ_DEV = 16
HEADS = 8
ROWS = 16
FEATS = HEADS * CHANNEL_SPAN
VALS = HEADS * ROWS
TOK = REQ_DEV * TS
LANES = 128
DECAY_AT = 2 * FEATS + VALS
LEARN_AT = DECAY_AT + LANES
WIDTH = LEARN_AT + LANES
F32 = jnp.float32
BF16 = jnp.bfloat16
FIRST_A, FIRST_B, FIRST_C, FIRST_D, FIRST_E, FIRST_F = 2, 19, 2, 2, 17, 10
VMEM = pl.BlockSpec(memory_space=pltpu.VMEM)
SMEM = pl.BlockSpec(memory_space=pltpu.SMEM)
ANY = pl.BlockSpec(memory_space=pl.ANY)


def value_lane(head, row):
    return (row % 2) * 64 + head * 8 + row // 2


def constant_matrices():
    lanes = np.arange(256)
    halves = (lanes[:, None] // 64 == lanes[None, :] // 64).astype(np.float32)
    c = np.arange(VALS)
    lane_head = (c % 64) // 8
    same_head = (lane_head[:, None] == lane_head[None, :]).astype(np.float32)
    head_to_lanes = (np.arange(FEATS)[:, None] // 64 == lane_head[None, :]).astype(np.float32)
    to_natural = np.zeros((VALS, VALS), np.float32)
    spread_values = np.zeros((FEATS, FEATS), np.float32)
    for head in range(HEADS):
        for row in range(ROWS):
            to_natural[value_lane(head, row), head * ROWS + row] = 1
            for part in range(4):
                spread_values[head * 64 + part * ROWS + row, part * VALS + value_lane(head, row)] = 1
    unpack = np.zeros((LANES, 2, LANES), np.float32)
    for side in range(2):
        unpack[side * 64:(side + 1) * 64, side] = same_head[side * 64:(side + 1) * 64]
    return halves, same_head, head_to_lanes, to_natural, spread_values, unpack.reshape(LANES, 256)


def dot(a, b):
    return jnp.dot(a, b, preferred_element_type=F32)


def dot_split(a, b):
    high = a.astype(BF16)
    low = (a - high.astype(F32)).astype(BF16)
    return dot(high, b) + dot(low, b)


def exchange(x, axes, first):
    order = [[k ^ first for k in range(x.shape[0])]] if first else None
    return lax.all_to_all(x, axes, 0, 0, tiled=True, axis_index_groups=order)


def call(kernel, outs, in_specs, args, scratch=(), flops=0, name=None, out_spec=VMEM):
    size = sum(int(np.prod(a.shape)) * a.dtype.itemsize for a in args)
    size += sum(int(np.prod(o.shape)) * o.dtype.itemsize for o in outs)
    single = len(outs) == 1
    return pl.pallas_call(
        kernel,
        out_shape=outs[0] if single else outs,
        in_specs=in_specs,
        out_specs=out_spec if single else [out_spec] * len(outs),
        scratch_shapes=list(scratch),
        cost_estimate=pl.CostEstimate(flops=flops, bytes_accessed=size, transcendentals=0),
        compiler_params=pltpu.CompilerParams(vmem_limit_bytes=32 * 2**20),
        name=name,
    )(*args)


def fan_kernel(x_ref, out_ref, done):
    copies = [pltpu.make_async_copy(x_ref, out_ref.at[at], done.at[at]) for at in range(4)]
    for copy in copies:
        copy.start()
    for copy in copies:
        copy.wait()


def pack_kernel(slot_ref, first_ref, x_ref, out_ref):
    for q in range(REQ_DEV):
        out_ref[(slot_ref[first_ref[0] + q] // REQ_DEV) ^ FIRST_B] = x_ref[q ^ (FIRST_A * 4)]


def mix_kernel(
    source_ref, count_ref, got_ref, shift_ref, blend_ref, proj_ref, decay_ref, learn_ref, value_ref,
    out_ref, new_shift_ref, tokens,
):
    for page in range(REQ_DEV):
        tile = got_ref[source_ref[page] ^ FIRST_B].astype(F32)
        for part in range(4):
            tokens[part, pl.ds(page, TS, stride=REQ_DEV), :] = tile[part * TS:(part + 1) * TS]
    current = jnp.concatenate([tokens[part] for part in range(4)], axis=1)
    before = jnp.concatenate([shift_ref[...], current[:-REQ_DEV]], axis=0)
    towards = before - current

    def mixed(branch):
        return (current + towards * blend_ref[branch:branch + 1, :]).astype(BF16)

    def low_rank(rows, weight):
        return lax.dot_general(
            rows, weight, (((1,), (1,)), ((), ())), preferred_element_type=F32
        ).astype(BF16)

    value = dot(mixed(3), value_ref[...]).astype(BF16)
    recept = dot(mixed(0), proj_ref[0]).astype(BF16)
    key = dot(mixed(2), proj_ref[1]).astype(BF16)
    decay = low_rank(mixed(1), decay_ref[...])
    learn = low_rank(mixed(4), learn_ref[...])
    pad = jnp.zeros((TOK, LANES - decay.shape[1]), BF16)
    for part in range(4):
        out_ref[part, :, 0:FEATS] = recept
        out_ref[part, :, FEATS:2 * FEATS] = key
        row = part ^ FIRST_C
        out_ref[part, :, 2 * FEATS:DECAY_AT] = value[:, row * VALS:(row + 1) * VALS]
        out_ref[part, :, DECAY_AT:LEARN_AT] = jnp.concatenate([decay, pad], axis=1)
        out_ref[part, :, LEARN_AT:WIDTH] = jnp.concatenate([learn, pad], axis=1)
    for page in range(REQ_DEV):
        row = (count_ref[page] - 1) * REQ_DEV + page
        for part in range(4):
            new_shift_ref[page:page + 1, part * LANES:(part + 1) * LANES] = tokens[part, pl.ds(row, 1), :]


def state_kernel(
    count_ref, got_ref, state_ref, decay_ref, decay_offset_ref, learn_ref, learn_offset_ref, gain_ref,
    correction_ref, reward_ref, halves_ref, same_head_ref, head_to_lanes_ref,
    new_state_ref, reading_ref, bonus_ref, stat_ref, spread, states, factors,
):
    lane = lax.broadcasted_iota(jnp.int32, (REQ_DEV, 256), 1)
    lane_key = lane % 64 - lane // 128
    for head in range(HEADS):
        for quad in range(4):
            at = (head * 4 + quad) * REQ_DEV
            for half in range(2):
                for group in range(2):
                    start = group * 512 + (quad * 2 + half) * 8 + head
                    states[at + group * 8:at + group * 8 + 8, half * LANES:(half + 1) * LANES] = (
                        state_ref[pl.ds(start, 8, stride=64), :]
                    )
    total = got_ref[0].astype(F32)
    for part in range(1, 4):
        total = total + got_ref[part].astype(F32)
    recept = total[:, 0:FEATS]
    key = total[:, FEATS:2 * FEATS]
    value = total[:, 2 * FEATS:DECAY_AT]
    decay_low = jnp.tanh(total[:, DECAY_AT:DECAY_AT + decay_ref.shape[0]]).astype(BF16)
    learn_low = total[:, LEARN_AT:LEARN_AT + learn_ref.shape[0]].astype(BF16)
    decay_in = decay_offset_ref[...] + dot(decay_low, decay_ref[...])
    learn = jax.nn.sigmoid(learn_offset_ref[...] + dot(learn_low, learn_ref[...]))
    decay = jnp.exp(jax.nn.sigmoid(decay_in) * (-float(np.exp(-0.5))))
    halves = halves_ref[...]
    scaled = key * gain_ref[...]
    squares = scaled * scaled
    norm = dot_split(jnp.concatenate([squares[:, 0:256], squares[:, 256:512]], axis=0), halves)
    norm = jnp.concatenate([norm[0:TOK], norm[TOK:2 * TOK]], axis=1)
    key_dir = scaled * lax.rsqrt(norm + 1e-6)
    key_adj = key * (1.0 + (learn - 1.0) * correction_ref[...])
    counts = count_ref[...]
    live = jnp.concatenate([jnp.where(counts > t, 1.0, 0.0) for t in range(TS)], axis=0)
    live_wide = jnp.concatenate([live] * 4, axis=1)
    vectors = [
        key_dir,
        jnp.where(live_wide > 0, decay, 1.0),
        key_dir * learn * live_wide,
        key_adj * live_wide,
        recept * live_wide,
    ]
    low_half = lax.broadcasted_iota(jnp.int32, (TOK, LANES), 1) < 64
    for at, vector in enumerate(vectors):
        for pair in range(HEADS // 2):
            block = vector[:, pair * LANES:(pair + 1) * LANES]
            turned = pltpu.roll(block, 64, 1)
            spread[at, 2 * pair] = jnp.where(low_half, block, turned)
            spread[at, 2 * pair + 1] = jnp.where(low_half, turned, block)
    value_pair = jnp.concatenate([value, value], axis=1)
    masks = [[lane_key == head * 8 + 2 * quad for quad in range(4)] for head in range(HEADS)]

    def vector_at(at, head, t):
        row = spread[at, head, t * REQ_DEV:(t + 1) * REQ_DEV, :]
        return jnp.concatenate([jnp.concatenate([row, row], axis=1)] * 4, axis=0)

    for t in range(TS + 1):
        for head in range(HEADS):
            place = slice(head * 64, (head + 1) * 64)
            state = states[place, :]
            if t > 0:
                removed = product[head * 64:(head + 1) * 64]
                added = product[512 + head * 64:512 + (head + 1) * 64]
                state = (
                    state * vector_at(1, head, t - 1)
                    - removed * vector_at(2, head, t - 1)
                    + added * vector_at(3, head, t - 1)
                )
                if t < TS:
                    states[place, :] = state
                else:
                    for quad in range(4):
                        for half in range(2):
                            for group in range(2):
                                at = quad * REQ_DEV + group * 8
                                start = group * 512 + (quad * 2 + half) * 8 + head
                                new_state_ref[pl.ds(start, 8, stride=64), :] = state[
                                    at:at + 8, half * LANES:(half + 1) * LANES
                                ]
                query = (state * vector_at(4, head, t - 1)).astype(BF16)
                factors[1024 + head * 64:1024 + (head + 1) * 64, :] = query
            if t < TS:
                factors[place, :] = (state * vector_at(0, head, t)).astype(BF16)
                now = value_pair[t * REQ_DEV:(t + 1) * REQ_DEV]
                picked = jnp.concatenate([jnp.where(m, now, 0.0) for m in masks[head]], axis=0)
                factors[512 + head * 64:512 + (head + 1) * 64, :] = picked.astype(BF16)
        first = 0 if t < TS else 1024
        last = 1536 if t > 0 else 1024
        product = dot(factors[first:last, :], halves)
        if t > 0:
            read = product[1024 - first:]
            reading = jnp.zeros((REQ_DEV, LANES), F32)
            for head in range(HEADS):
                for quad in range(4):
                    at = (head * 4 + quad) * REQ_DEV
                    part = jnp.where(masks[head][quad], read[at:at + REQ_DEV], 0.0)
                    reading = reading + part[:, 0:LANES] + part[:, LANES:256]
            reading_ref[(t - 1) * REQ_DEV:t * REQ_DEV, :] = reading
    reward = dot_split(recept * key_adj * reward_ref[...], head_to_lanes_ref[...])
    bonus_ref[...] = reward * value * live
    reading = reading_ref[...]
    same_head = same_head_ref[...]
    head_sum = dot_split(reading, same_head)
    away = reading - head_sum * (1.0 / ROWS)
    away_sum = dot_split(away * away, same_head)
    stat = jnp.where(low_half, head_sum, away_sum)
    slot = lax.broadcasted_iota(jnp.int32, (8, LANES), 1) % 8
    packed = jnp.zeros((8, LANES), F32)
    for group in range(8):
        packed = packed + jnp.where(slot == group, stat[group * 8:(group + 1) * 8], 0.0)
    for part in range(4):
        stat_ref[part] = packed


def norm_kernel(source_ref, stat_ref, reading_ref, bonus_ref, gain_ref, unpack_ref, out_ref, rows):
    lane = lax.broadcasted_iota(jnp.int32, (8, LANES), 1)
    stats = [stat_ref[part] for part in range(4)]
    mean = (stats[0] + stats[1] + stats[2] + stats[3]) * (1.0 / CHANNEL_SPAN)
    away = pltpu.roll(stats[0] + stats[1] + stats[2] + stats[3], 64, 1)
    for part in range(4):
        gap = stats[part] * (1.0 / ROWS) - mean
        away = away + gap * gap * float(ROWS)
    scale = lax.rsqrt(jnp.where(lane < 64, away, 0.0) * (1.0 / CHANNEL_SPAN) + 0.00064)
    both = jnp.where(lane < 64, mean, pltpu.roll(scale, 64, 1))
    packed = jnp.concatenate([jnp.where(lane % 8 == group, both, 0.0) for group in range(8)], axis=0)
    high = packed.astype(BF16)
    rest = packed - high.astype(F32)
    middle = rest.astype(BF16)
    low = (rest - middle.astype(F32)).astype(BF16)
    opened = dot(jnp.concatenate([high, middle, low], axis=0), unpack_ref[...])
    opened = opened[0:TOK] + opened[TOK:2 * TOK] + opened[2 * TOK:3 * TOK]
    normed = (reading_ref[...] - opened[:, 0:LANES]) * opened[:, LANES:256] * gain_ref[...] + bonus_ref[...]
    rows[...] = normed
    for page in range(REQ_DEV):
        out_ref[source_ref[page] ^ FIRST_E] = rows[pl.ds(page, TS, stride=REQ_DEV), :].astype(BF16)


def output_kernel(slot_ref, first_ref, got_ref, proj_ref, out_ref, rows):
    for q in range(REQ_DEV):
        rows[q * TS:(q + 1) * TS, :] = got_ref[
            (slot_ref[first_ref[0] + q] // REQ_DEV) ^ FIRST_E
        ].astype(F32)
    terms = dot(rows[...].astype(BF16), proj_ref[...]).astype(BF16)
    for head in range(4):
        for part in range(4):
            out_ref[(head * 4 + part) ^ FIRST_F] = terms[
                head * REQ_DEV:(head + 1) * REQ_DEV, part * FEATS:(part + 1) * FEATS
            ]


def shaped(shape, dtype):
    return jax.ShapeDtypeStruct(shape, dtype)


def per_device(
    incoming_activations,
    genuine_symbol_number,
    caller_sheet_slot,
    memory_sheets,
    prior_activation_sheets,
    blend_fractions,
    first_projectors,
    fading_narrow_projector,
    fading_widen_projector,
    fading_offset,
    context_step_narrowing,
    context_step_widening,
    context_step_offset,
    erasure_address_gain,
    address_correction,
    reward_coefficients,
    groupwise_gain,
    final_projector,
):
    groups = lax.axis_size("req")
    halves, same_head, head_to_lanes, to_natural, spread_values, unpack = [
        jnp.asarray(m, BF16) for m in constant_matrices()
    ]
    first = lax.axis_index("req") * REQ_DEV
    pages = first + jnp.arange(REQ_DEV, dtype=jnp.int32)
    holder = caller_sheet_slot[None, :] == pages[:, None]
    groups_of = lax.shift_right_logical(jnp.arange(caller_sheet_slot.shape[0], dtype=jnp.int32), 4)
    source = jnp.sum(jnp.where(holder, groups_of[None, :], 0), axis=1)
    count = jnp.sum(jnp.where(holder, genuine_symbol_number[None, :], 0), axis=1)
    count_wide = jnp.broadcast_to(count[:, None], (REQ_DEV, LANES))
    first = first.astype(jnp.int32)[None]
    gain = groupwise_gain.reshape(HEADS, 8, 2).transpose(2, 0, 1).reshape(1, VALS)
    reward = reward_coefficients.reshape(1, FEATS)

    tiles = incoming_activations.reshape(4, TS, 4, LANES).transpose(0, 2, 1, 3).reshape(4, 16, LANES)
    everywhere = call(
        fan_kernel,
        [shaped((4, 4, 16, LANES), BF16)],
        [pl.BlockSpec(memory_space=pltpu.HBM)],
        (tiles,),
        scratch=[pltpu.SemaphoreType.DMA((4,))],
        flops=6 * 10**9,
        name="fan",
        out_spec=ANY,
    )
    mine = exchange(everywhere, "head", FIRST_A).reshape(REQ_DEV, 16, LANES)
    value_projector = dot(first_projectors[2], spread_values).astype(BF16)
    output_projector = dot(to_natural, final_projector.reshape(VALS, 4 * FEATS)).astype(BF16)
    mine, source, count, count_wide, gain, reward, value_projector, output_projector = (
        lax.optimization_barrier(
            (mine, source, count, count_wide, gain, reward, value_projector, output_projector)
        )
    )
    packed = call(
        pack_kernel,
        [shaped((groups, 16, LANES), BF16)],
        [SMEM, SMEM, VMEM],
        (caller_sheet_slot, first, mine),
        flops=6 * 10**9,
        name="pack",
    )
    got = exchange(packed, "req", FIRST_B)
    partial, new_shift = call(
        mix_kernel,
        [shaped((4, TOK, WIDTH), BF16), shaped((REQ_DEV, FEATS), F32)],
        [SMEM] * 2 + [VMEM] * 7,
        (
            source, count, got, prior_activation_sheets, blend_fractions, first_projectors,
            fading_narrow_projector.T, context_step_narrowing.T, value_projector,
        ),
        scratch=[pltpu.VMEM((4, TOK, LANES), F32)],
        flops=2 * TOK * FEATS * (3 * FEATS + 192),
        name="mix",
    )
    sheets = memory_sheets.reshape(REQ_DEV, HEADS, 8, LANES).transpose(0, 2, 1, 3)
    sheets = sheets.reshape(REQ_DEV * HEADS * 8, LANES)
    sums = exchange(partial, "row", FIRST_C)
    new_state, reading, bonus, stat = call(
        state_kernel,
        [
            shaped((REQ_DEV * HEADS * 8, LANES), F32),
            shaped((TOK, LANES), F32),
            shaped((TOK, LANES), F32),
            shaped((4, 8, LANES), F32),
        ],
        [VMEM] * 13,
        (
            count_wide,
            sums,
            sheets,
            fading_widen_projector,
            fading_offset[None],
            context_step_widening,
            context_step_offset[None],
            erasure_address_gain[None],
            address_correction[None],
            reward,
            halves,
            same_head,
            head_to_lanes,
        ),
        scratch=[pltpu.VMEM((5, HEADS, TOK, LANES), F32), pltpu.VMEM((512, 256), F32), pltpu.VMEM((1536, 256), BF16)],
        flops=2 * 3 * TS * 512 * 256 * 256,
        name="state",
    )
    stats = exchange(stat, "row", FIRST_D)
    leaving = call(
        norm_kernel,
        [shaped((groups, TS, LANES), BF16)],
        [SMEM] + [VMEM] * 5,
        (source, stats, reading, bonus, gain, unpack),
        scratch=[pltpu.VMEM((TOK, LANES), F32)],
        name="norm",
    )
    back = exchange(leaving, "req", FIRST_E)
    terms = call(
        output_kernel,
        [shaped((16, 16, FEATS), BF16)],
        [SMEM, SMEM, VMEM, VMEM],
        (caller_sheet_slot, first, back, output_projector),
        scratch=[pltpu.VMEM((TOK, LANES), F32)],
        flops=2 * TOK * VALS * 4 * FEATS,
        name="output",
    )
    arrived = exchange(terms, ("head", "row"), FIRST_F)
    mixed = jnp.sum(arrived.astype(F32), axis=0).astype(BF16).reshape(4, TS, FEATS)
    new_state = new_state.reshape(REQ_DEV, 8, HEADS, LANES).transpose(0, 2, 1, 3)
    return (mixed, new_state.reshape(REQ_DEV, HEADS, 8 * LANES), new_shift)


def solution(mesh):
    placed = (
        P(("req", "head"), None, "row"),
        P(),
        P(),
        P("req", "head", "row"),
        P("req", "row"),
        P(None, "row"),
        P(None, "row", "head"),
        P("row", None),
        P(None, "head"),
        P("head"),
        P("row", None),
        P(None, "head"),
        P("head"),
        P("head"),
        P("head"),
        P("head", None),
        P("head", "row"),
        P("head", "row", None),
    )
    return jax.shard_map(
        per_device,
        mesh=mesh,
        in_specs=placed,
        out_specs=(P(("req", "head"), None, "row"), P("req", "head", "row"), P("req", "row")),
        check_vma=False,
    )
```

```python
import functools

import jax
import jax.numpy as jnp
import numpy as np
from jax import lax
from jax.experimental import pallas as pl
from jax.experimental.pallas import tpu as pltpu
from jax.sharding import PartitionSpec as P

CHANNEL_SPAN = 64
TS = 4
REQ_DEV = 16
HEADS = 8
ROWS = 16
FEATS = HEADS * CHANNEL_SPAN
VALS = HEADS * ROWS
TOK = REQ_DEV * TS
LANES = 128
DECAY_AT = 2 * FEATS + VALS
LEARN_AT = DECAY_AT + LANES
WIDTH = LEARN_AT + LANES
F32 = jnp.float32
BF16 = jnp.bfloat16
FIRST_A, FIRST_B, FIRST_C, FIRST_D, FIRST_E, FIRST_F = 2, 19, 2, 2, 17, 10
VMEM = pl.BlockSpec(memory_space=pltpu.VMEM)
SMEM = pl.BlockSpec(memory_space=pltpu.SMEM)
ANY = pl.BlockSpec(memory_space=pl.ANY)


def value_lane(head, row):
    return (row % 2) * 64 + head * 8 + row // 2


def constant_matrices():
    lanes = np.arange(256)
    halves = (lanes[:, None] // 64 == lanes[None, :] // 64).astype(np.float32)
    c = np.arange(VALS)
    lane_head = (c % 64) // 8
    same_head = (lane_head[:, None] == lane_head[None, :]).astype(np.float32)
    head_to_lanes = (np.arange(FEATS)[:, None] // 64 == lane_head[None, :]).astype(np.float32)
    to_natural = np.zeros((VALS, VALS), np.float32)
    spread_values = np.zeros((FEATS, FEATS), np.float32)
    for head in range(HEADS):
        for row in range(ROWS):
            to_natural[value_lane(head, row), head * ROWS + row] = 1
            for part in range(4):
                spread_values[head * 64 + part * ROWS + row, part * VALS + value_lane(head, row)] = 1
    unpack = np.zeros((LANES, 2, LANES), np.float32)
    for side in range(2):
        unpack[side * 64:(side + 1) * 64, side] = same_head[side * 64:(side + 1) * 64]
    return halves, same_head, head_to_lanes, to_natural, spread_values, unpack.reshape(LANES, 256)


def dot(a, b):
    return jnp.dot(a, b, preferred_element_type=F32)


def dot_split(a, b):
    high = a.astype(BF16)
    low = (a - high.astype(F32)).astype(BF16)
    return dot(high, b) + dot(low, b)


def exchange(x, axes, first):
    order = [[k ^ first for k in range(x.shape[0])]] if first else None
    return lax.all_to_all(x, axes, 0, 0, tiled=True, axis_index_groups=order)


def call(kernel, outs, in_specs, args, scratch=(), flops=0, name=None, out_spec=VMEM):
    size = sum(int(np.prod(a.shape)) * a.dtype.itemsize for a in args)
    size += sum(int(np.prod(o.shape)) * o.dtype.itemsize for o in outs)
    single = len(outs) == 1
    return pl.pallas_call(
        kernel,
        out_shape=outs[0] if single else outs,
        in_specs=in_specs,
        out_specs=out_spec if single else [out_spec] * len(outs),
        scratch_shapes=list(scratch),
        cost_estimate=pl.CostEstimate(flops=flops, bytes_accessed=size, transcendentals=0),
        compiler_params=pltpu.CompilerParams(vmem_limit_bytes=32 * 2**20),
        name=name,
    )(*args)


def fan_kernel(x_ref, out_ref, done):
    copies = [pltpu.make_async_copy(x_ref, out_ref.at[at], done.at[at]) for at in range(4)]
    for copy in copies:
        copy.start()
    for copy in copies:
        copy.wait()


def pack_kernel(slot_ref, first_ref, x_ref, out_ref):
    for q in range(REQ_DEV):
        out_ref[(slot_ref[first_ref[0] + q] // REQ_DEV) ^ FIRST_B] = x_ref[q ^ (FIRST_A * 4)]


def mix_kernel(
    source_ref, count_ref, got_ref, shift_ref, blend_ref, proj_ref, decay_ref, learn_ref, value_ref,
    out_ref, new_shift_ref, tokens,
):
    for page in range(REQ_DEV):
        tile = got_ref[source_ref[page] ^ FIRST_B].astype(F32)
        for part in range(4):
            tokens[part, pl.ds(page, TS, stride=REQ_DEV), :] = tile[part * TS:(part + 1) * TS]
    current = jnp.concatenate([tokens[part] for part in range(4)], axis=1)
    before = jnp.concatenate([shift_ref[...], current[:-REQ_DEV]], axis=0)
    towards = before - current

    def mixed(branch):
        return (current + towards * blend_ref[branch:branch + 1, :]).astype(BF16)

    def low_rank(rows, weight):
        return lax.dot_general(
            rows, weight, (((1,), (1,)), ((), ())), preferred_element_type=F32
        ).astype(BF16)

    value = dot(mixed(3), value_ref[...]).astype(BF16)
    recept = dot(mixed(0), proj_ref[0]).astype(BF16)
    key = dot(mixed(2), proj_ref[1]).astype(BF16)
    decay = low_rank(mixed(1), decay_ref[...])
    learn = low_rank(mixed(4), learn_ref[...])
    pad = jnp.zeros((TOK, LANES - decay.shape[1]), BF16)
    for part in range(4):
        out_ref[part, :, 0:FEATS] = recept
        out_ref[part, :, FEATS:2 * FEATS] = key
        row = part ^ FIRST_C
        out_ref[part, :, 2 * FEATS:DECAY_AT] = value[:, row * VALS:(row + 1) * VALS]
        out_ref[part, :, DECAY_AT:LEARN_AT] = jnp.concatenate([decay, pad], axis=1)
        out_ref[part, :, LEARN_AT:WIDTH] = jnp.concatenate([learn, pad], axis=1)
    for page in range(REQ_DEV):
        row = (count_ref[page] - 1) * REQ_DEV + page
        for part in range(4):
            new_shift_ref[page:page + 1, part * LANES:(part + 1) * LANES] = tokens[part, pl.ds(row, 1), :]


def order_kernel(state_ref, states):
    for head in range(HEADS):
        for quad in range(4):
            at = (head * 4 + quad) * REQ_DEV
            for half in range(2):
                for group in range(2):
                    start = group * 512 + (quad * 2 + half) * 8 + head
                    states[at + group * 8:at + group * 8 + 8, half * LANES:(half + 1) * LANES] = (
                        state_ref[pl.ds(start, 8, stride=64), :]
                    )


def state_kernel(
    count_ref, got_ref, state_ref, decay_ref, decay_offset_ref, learn_ref, learn_offset_ref, gain_ref,
    correction_ref, reward_ref, halves_ref, same_head_ref, head_to_lanes_ref,
    new_state_ref, reading_ref, bonus_ref, stat_ref, spread, states, factors,
):
    lane = lax.broadcasted_iota(jnp.int32, (REQ_DEV, 256), 1)
    lane_key = lane % 64 - lane // 128
    total = got_ref[0].astype(F32)
    for part in range(1, 4):
        total = total + got_ref[part].astype(F32)
    recept = total[:, 0:FEATS]
    key = total[:, FEATS:2 * FEATS]
    value = total[:, 2 * FEATS:DECAY_AT]
    decay_low = jnp.tanh(total[:, DECAY_AT:DECAY_AT + decay_ref.shape[0]]).astype(BF16)
    learn_low = total[:, LEARN_AT:LEARN_AT + learn_ref.shape[0]].astype(BF16)
    decay_in = decay_offset_ref[...] + dot(decay_low, decay_ref[...])
    learn = jax.nn.sigmoid(learn_offset_ref[...] + dot(learn_low, learn_ref[...]))
    decay = jnp.exp(jax.nn.sigmoid(decay_in) * (-float(np.exp(-0.5))))
    halves = halves_ref[...]
    scaled = key * gain_ref[...]
    squares = scaled * scaled
    norm = dot_split(jnp.concatenate([squares[:, 0:256], squares[:, 256:512]], axis=0), halves)
    norm = jnp.concatenate([norm[0:TOK], norm[TOK:2 * TOK]], axis=1)
    key_dir = scaled * lax.rsqrt(norm + 1e-6)
    key_adj = key * (1.0 + (learn - 1.0) * correction_ref[...])
    counts = count_ref[...]
    live = jnp.concatenate([jnp.where(counts > t, 1.0, 0.0) for t in range(TS)], axis=0)
    live_wide = jnp.concatenate([live] * 4, axis=1)
    vectors = [
        key_dir,
        jnp.where(live_wide > 0, decay, 1.0),
        key_dir * learn * live_wide,
        key_adj * live_wide,
        recept * live_wide,
    ]
    low_half = lax.broadcasted_iota(jnp.int32, (TOK, LANES), 1) < 64
    for at, vector in enumerate(vectors):
        for pair in range(HEADS // 2):
            block = vector[:, pair * LANES:(pair + 1) * LANES]
            turned = pltpu.roll(block, 64, 1)
            spread[at, 2 * pair] = jnp.where(low_half, block, turned)
            spread[at, 2 * pair + 1] = jnp.where(low_half, turned, block)
    value_pair = jnp.concatenate([value, value], axis=1)
    masks = [[lane_key == head * 8 + 2 * quad for quad in range(4)] for head in range(HEADS)]

    def vector_at(at, head, t):
        row = spread[at, head, t * REQ_DEV:(t + 1) * REQ_DEV, :]
        return jnp.concatenate([jnp.concatenate([row, row], axis=1)] * 4, axis=0)

    for t in range(TS + 1):
        for head in range(HEADS):
            place = slice(head * 64, (head + 1) * 64)
            state = states[place, :] if t > 0 else state_ref[place, :]
            if t > 0:
                removed = product[head * 64:(head + 1) * 64]
                added = product[512 + head * 64:512 + (head + 1) * 64]
                state = (
                    state * vector_at(1, head, t - 1)
                    - removed * vector_at(2, head, t - 1)
                    + added * vector_at(3, head, t - 1)
                )
                if t < TS:
                    states[place, :] = state
                else:
                    for quad in range(4):
                        for half in range(2):
                            for group in range(2):
                                at = quad * REQ_DEV + group * 8
                                start = group * 512 + (quad * 2 + half) * 8 + head
                                new_state_ref[pl.ds(start, 8, stride=64), :] = state[
                                    at:at + 8, half * LANES:(half + 1) * LANES
                                ]
                query = (state * vector_at(4, head, t - 1)).astype(BF16)
                factors[1024 + head * 64:1024 + (head + 1) * 64, :] = query
            else:
                states[place, :] = state
            if t < TS:
                factors[place, :] = (state * vector_at(0, head, t)).astype(BF16)
                now = value_pair[t * REQ_DEV:(t + 1) * REQ_DEV]
                picked = jnp.concatenate([jnp.where(m, now, 0.0) for m in masks[head]], axis=0)
                factors[512 + head * 64:512 + (head + 1) * 64, :] = picked.astype(BF16)
        first = 0 if t < TS else 1024
        last = 1536 if t > 0 else 1024
        product = dot(factors[first:last, :], halves)
        if t > 0:
            read = product[1024 - first:]
            reading = jnp.zeros((REQ_DEV, LANES), F32)
            for head in range(HEADS):
                for quad in range(4):
                    at = (head * 4 + quad) * REQ_DEV
                    part = jnp.where(masks[head][quad], read[at:at + REQ_DEV], 0.0)
                    reading = reading + part[:, 0:LANES] + part[:, LANES:256]
            reading_ref[(t - 1) * REQ_DEV:t * REQ_DEV, :] = reading
    reward = dot_split(recept * key_adj * reward_ref[...], head_to_lanes_ref[...])
    bonus_ref[...] = reward * value * live
    reading = reading_ref[...]
    same_head = same_head_ref[...]
    head_sum = dot_split(reading, same_head)
    away = reading - head_sum * (1.0 / ROWS)
    away_sum = dot_split(away * away, same_head)
    stat = jnp.where(low_half, head_sum, away_sum)
    slot = lax.broadcasted_iota(jnp.int32, (8, LANES), 1) % 8
    packed = jnp.zeros((8, LANES), F32)
    for group in range(8):
        packed = packed + jnp.where(slot == group, stat[group * 8:(group + 1) * 8], 0.0)
    for part in range(4):
        stat_ref[part] = packed


def norm_kernel(source_ref, stat_ref, reading_ref, bonus_ref, gain_ref, unpack_ref, out_ref, rows):
    lane = lax.broadcasted_iota(jnp.int32, (8, LANES), 1)
    stats = [stat_ref[part] for part in range(4)]
    mean = (stats[0] + stats[1] + stats[2] + stats[3]) * (1.0 / CHANNEL_SPAN)
    away = pltpu.roll(stats[0] + stats[1] + stats[2] + stats[3], 64, 1)
    for part in range(4):
        gap = stats[part] * (1.0 / ROWS) - mean
        away = away + gap * gap * float(ROWS)
    scale = lax.rsqrt(jnp.where(lane < 64, away, 0.0) * (1.0 / CHANNEL_SPAN) + 0.00064)
    both = jnp.where(lane < 64, mean, pltpu.roll(scale, 64, 1))
    packed = jnp.concatenate([jnp.where(lane % 8 == group, both, 0.0) for group in range(8)], axis=0)
    high = packed.astype(BF16)
    rest = packed - high.astype(F32)
    middle = rest.astype(BF16)
    low = (rest - middle.astype(F32)).astype(BF16)
    opened = dot(jnp.concatenate([high, middle, low], axis=0), unpack_ref[...])
    opened = opened[0:TOK] + opened[TOK:2 * TOK] + opened[2 * TOK:3 * TOK]
    normed = (reading_ref[...] - opened[:, 0:LANES]) * opened[:, LANES:256] * gain_ref[...] + bonus_ref[...]
    rows[...] = normed
    for page in range(REQ_DEV):
        out_ref[source_ref[page] ^ FIRST_E] = rows[pl.ds(page, TS, stride=REQ_DEV), :].astype(BF16)


def output_kernel(slot_ref, first_ref, got_ref, proj_ref, out_ref, rows):
    for q in range(REQ_DEV):
        rows[q * TS:(q + 1) * TS, :] = got_ref[
            (slot_ref[first_ref[0] + q] // REQ_DEV) ^ FIRST_E
        ].astype(F32)
    terms = dot(rows[...].astype(BF16), proj_ref[...]).astype(BF16)
    for head in range(4):
        for part in range(4):
            out_ref[(head * 4 + part) ^ FIRST_F] = terms[
                head * REQ_DEV:(head + 1) * REQ_DEV, part * FEATS:(part + 1) * FEATS
            ]


def shaped(shape, dtype):
    return jax.ShapeDtypeStruct(shape, dtype)


def per_device(
    incoming_activations,
    genuine_symbol_number,
    caller_sheet_slot,
    memory_sheets,
    prior_activation_sheets,
    blend_fractions,
    first_projectors,
    fading_narrow_projector,
    fading_widen_projector,
    fading_offset,
    context_step_narrowing,
    context_step_widening,
    context_step_offset,
    erasure_address_gain,
    address_correction,
    reward_coefficients,
    groupwise_gain,
    final_projector,
):
    groups = lax.axis_size("req")
    halves, same_head, head_to_lanes, to_natural, spread_values, unpack = [
        jnp.asarray(m, BF16) for m in constant_matrices()
    ]
    first = lax.axis_index("req") * REQ_DEV
    pages = first + jnp.arange(REQ_DEV, dtype=jnp.int32)
    holder = caller_sheet_slot[None, :] == pages[:, None]
    groups_of = lax.shift_right_logical(jnp.arange(caller_sheet_slot.shape[0], dtype=jnp.int32), 4)
    source = jnp.sum(jnp.where(holder, groups_of[None, :], 0), axis=1)
    count = jnp.sum(jnp.where(holder, genuine_symbol_number[None, :], 0), axis=1)
    count_wide = jnp.broadcast_to(count[:, None], (REQ_DEV, LANES))
    first = first.astype(jnp.int32)[None]
    gain = groupwise_gain.reshape(HEADS, 8, 2).transpose(2, 0, 1).reshape(1, VALS)
    reward = reward_coefficients.reshape(1, FEATS)

    tiles = incoming_activations.reshape(4, TS, 4, LANES).transpose(0, 2, 1, 3).reshape(4, 16, LANES)
    everywhere = call(
        fan_kernel,
        [shaped((4, 4, 16, LANES), BF16)],
        [pl.BlockSpec(memory_space=pltpu.HBM)],
        (tiles,),
        scratch=[pltpu.SemaphoreType.DMA((4,))],
        flops=6 * 10**9,
        name="fan",
        out_spec=ANY,
    )
    mine = exchange(everywhere, "head", FIRST_A).reshape(REQ_DEV, 16, LANES)
    sheets = memory_sheets.reshape(REQ_DEV, HEADS, 8, LANES).transpose(0, 2, 1, 3)
    sheets = sheets.reshape(REQ_DEV * HEADS * 8, LANES)
    sheets = call(order_kernel, [shaped((512, 256), F32)], [VMEM], (sheets,), name="order")
    value_projector = dot(first_projectors[2], spread_values).astype(BF16)
    output_projector = dot(to_natural, final_projector.reshape(VALS, 4 * FEATS)).astype(BF16)
    mine, source, count, count_wide, gain, reward, value_projector, output_projector, sheets = (
        lax.optimization_barrier(
            (mine, source, count, count_wide, gain, reward, value_projector, output_projector, sheets)
        )
    )
    packed = call(
        pack_kernel,
        [shaped((groups, 16, LANES), BF16)],
        [SMEM, SMEM, VMEM],
        (caller_sheet_slot, first, mine),
        flops=6 * 10**9,
        name="pack",
    )
    got = exchange(packed, "req", FIRST_B)
    partial, new_shift = call(
        mix_kernel,
        [shaped((4, TOK, WIDTH), BF16), shaped((REQ_DEV, FEATS), F32)],
        [SMEM] * 2 + [VMEM] * 7,
        (
            source, count, got, prior_activation_sheets, blend_fractions, first_projectors,
            fading_narrow_projector.T, context_step_narrowing.T, value_projector,
        ),
        scratch=[pltpu.VMEM((4, TOK, LANES), F32)],
        flops=2 * TOK * FEATS * (3 * FEATS + 192),
        name="mix",
    )
    sums = exchange(partial, "row", FIRST_C)
    new_state, reading, bonus, stat = call(
        state_kernel,
        [
            shaped((REQ_DEV * HEADS * 8, LANES), F32),
            shaped((TOK, LANES), F32),
            shaped((TOK, LANES), F32),
            shaped((4, 8, LANES), F32),
        ],
        [VMEM] * 13,
        (
            count_wide,
            sums,
            sheets,
            fading_widen_projector,
            fading_offset[None],
            context_step_widening,
            context_step_offset[None],
            erasure_address_gain[None],
            address_correction[None],
            reward,
            halves,
            same_head,
            head_to_lanes,
        ),
        scratch=[pltpu.VMEM((5, HEADS, TOK, LANES), F32), pltpu.VMEM((512, 256), F32), pltpu.VMEM((1536, 256), BF16)],
        flops=2 * 3 * TS * 512 * 256 * 256,
        name="state",
    )
    stats = exchange(stat, "row", FIRST_D)
    leaving = call(
        norm_kernel,
        [shaped((groups, TS, LANES), BF16)],
        [SMEM] + [VMEM] * 5,
        (source, stats, reading, bonus, gain, unpack),
        scratch=[pltpu.VMEM((TOK, LANES), F32)],
        name="norm",
    )
    back = exchange(leaving, "req", FIRST_E)
    terms = call(
        output_kernel,
        [shaped((16, 16, FEATS), BF16)],
        [SMEM, SMEM, VMEM, VMEM],
        (caller_sheet_slot, first, back, output_projector),
        scratch=[pltpu.VMEM((TOK, LANES), F32)],
        flops=2 * TOK * VALS * 4 * FEATS,
        name="output",
    )
    arrived = exchange(terms, ("head", "row"), FIRST_F)
    mixed = jnp.sum(arrived.astype(F32), axis=0).astype(BF16).reshape(4, TS, FEATS)
    new_state = new_state.reshape(REQ_DEV, 8, HEADS, LANES).transpose(0, 2, 1, 3)
    return (mixed, new_state.reshape(REQ_DEV, HEADS, 8 * LANES), new_shift)


def solution(mesh):
    placed = (
        P(("req", "head"), None, "row"),
        P(),
        P(),
        P("req", "head", "row"),
        P("req", "row"),
        P(None, "row"),
        P(None, "row", "head"),
        P("row", None),
        P(None, "head"),
        P("head"),
        P("row", None),
        P(None, "head"),
        P("head"),
        P("head"),
        P("head"),
        P("head", None),
        P("head", "row"),
        P("head", "row", None),
    )
    return jax.shard_map(
        per_device,
        mesh=mesh,
        in_specs=placed,
        out_specs=(P(("req", "head"), None, "row"), P("req", "head", "row"), P("req", "row")),
        check_vma=False,
    )
```
